128 devices in a mesh: amp: 128 (over y, x, z, core).
Axes of the slice: x: 4, y: 4, z: 4, core: 2. Of those that a mesh axis runs over, the one named last changes fastest.
Arguments:
- state: float32 [2, 16777216], P(None, 'amp'), may hold values from -6 to 6
- costate: float32 [2, 16777216], P(None, 'amp'), may hold values from -6 to 6
- gates: float32 [3, 2, 128, 128], replicated, may hold values from -1 to 1, as said below
Outputs:
- state_out: float32 [2, 16777216], P(None, 'amp')
- costate_out: float32 [2, 16777216], P(None, 'amp')
- gradients: float32 [3, 2, 128, 128], replicated
The draws below stay inside these ranges and needn't reach their ends.
Inputs may be any that keep to these rules, and one draw needn't show every extreme that they name: Each gates[l, 0] + i gates[l, 1] is a unitary matrix.
All inputs are finite; a program needn't handle non-finite values.
Results may differ from the reference program's by a relative error of at most 0.0001.
Values sent between devices are 32-bit elements; how exact they have to be, the bound alone decides.
A program may use at most 64 MiB of HBM per device.

```python
import math
import jax
import jax.numpy as jnp
from jax import lax

GATE = 128
LAYERS = 3
AMP_DEV = 131072
STATE = 16777216
N_AMP = 128


def draw_gates(key, part):
    key_real, key_imag = jax.random.split(jax.random.fold_in(key, 17))
    real_part = jax.random.normal(key_real, (LAYERS, GATE, GATE), jnp.float32)
    imag_part = jax.random.normal(key_imag, (LAYERS, GATE, GATE), jnp.float32)
    matrix = lax.complex(real_part, imag_part)
    factor_q, factor_r = jnp.linalg.qr(matrix)
    diagonal = jnp.diagonal(factor_r, axis1=-2, axis2=-1)
    phases = diagonal / jnp.abs(diagonal)
    unitary = factor_q * phases[:, None, :]
    return jnp.stack([jnp.real(unitary), jnp.imag(unitary)], axis=1).astype(jnp.float32)


def block_scale(stream_key, dims, cuts, low, top_value):
    gain = 1.0
    for position, parts in cuts:
        heights = jax.random.uniform(jax.random.fold_in(jax.random.fold_in(stream_key, 6), position), (parts,), jnp.float32, low / len(cuts), top_value / len(cuts))
        gain = gain * jnp.repeat(jnp.exp(heights), dims[position] // parts).reshape((-1,) + (1,) * (len(dims) - 1 - position))
    return gain


def bell_draw(key, extent, width, reach, shards=(), kind=jnp.bfloat16):
    gain = block_scale(key, extent, shards, -0.22, 0.18) if shards else 1.0
    result = jax.random.normal(key, extent, jnp.float32) * width * gain
    return jnp.minimum(jnp.maximum(result, -reach), reach).astype(kind)


def setup_inputs(seed: int = 0) -> dict:
    seeds = jax.random.split(jax.random.key(seed), 4)
    state = bell_draw(seeds[0], (2, STATE), 1.0, 6.0, ((1, 128),), jnp.float32)
    costate = bell_draw(seeds[1], (2, STATE), 1.0, 6.0, ((1, 128),), jnp.float32)
    gates = draw_gates(jax.random.fold_in(seeds[3], 71), 0)
    return dict(state=state, costate=costate, gates=gates)


def undo_gate(field, gate_now):
    gate_real = gate_now[0]
    gate_imag = gate_now[1]
    high = lax.Precision.HIGHEST
    new_real = jnp.einsum('ts,dtc->dsc', gate_real, field[0], precision=high) + jnp.einsum('ts,dtc->dsc', gate_imag, field[1], precision=high)
    new_imag = jnp.einsum('ts,dtc->dsc', gate_real, field[1], precision=high) - jnp.einsum('ts,dtc->dsc', gate_imag, field[0], precision=high)
    return jnp.stack([new_real, new_imag], axis=0)

def gate_gradient(adjoint, amplitudes):
    high = lax.Precision.HIGHEST
    grad_real = jnp.einsum('dtc,dsc->ts', adjoint[0], amplitudes[0], precision=high) + jnp.einsum('dtc,dsc->ts', adjoint[1], amplitudes[1], precision=high)
    grad_imag = jnp.einsum('dtc,dsc->ts', adjoint[1], amplitudes[0], precision=high) - jnp.einsum('dtc,dsc->ts', adjoint[0], amplitudes[1], precision=high)
    return jnp.stack([grad_real, grad_imag], axis=0)

def swap_bits(field, dev_bit, gate_bit):
    shape_now = field.shape
    reshaped = field.reshape(2, shape_now[1] >> dev_bit + 1, 2, 1 << dev_bit, shape_now[2] >> gate_bit + 1, 2, (1 << gate_bit) * shape_now[3])
    return jnp.swapaxes(reshaped, 2, 5).reshape(shape_now)

def regroup_bits(field):
    shape_now = field.shape
    reshaped = field.reshape(2, shape_now[1], shape_now[2] // shape_now[1], shape_now[1], shape_now[3])
    return jnp.swapaxes(reshaped, 1, 3).reshape(shape_now)

def reference(state, costate, gates):
    columns = AMP_DEV // GATE
    amplitudes = state.reshape(2, N_AMP, GATE, columns)
    adjoint = costate.reshape(2, N_AMP, GATE, columns)
    device_bits = N_AMP.bit_length() - 1
    gate_bits = GATE.bit_length() - 1
    grad_scale = 1.0 / math.sqrt(STATE // GATE)
    gradient_list = []
    for layer_index in range(LAYERS):
        amplitudes = undo_gate(amplitudes, gates[layer_index])
        gradient_list.append(gate_gradient(adjoint, amplitudes) * grad_scale)
        adjoint = undo_gate(adjoint, gates[layer_index])
        if layer_index + 1 < LAYERS:
            if layer_index % 2 == 0:
                amplitudes = swap_bits(amplitudes, device_bits - 1, gate_bits - 1)
                adjoint = swap_bits(adjoint, device_bits - 1, gate_bits - 1)
                amplitudes = swap_bits(amplitudes, 0, gate_bits - 2)
                adjoint = swap_bits(adjoint, 0, gate_bits - 2)
            else:
                amplitudes = regroup_bits(amplitudes)
                adjoint = regroup_bits(adjoint)
    return (amplitudes.reshape(2, STATE), adjoint.reshape(2, STATE), jnp.stack(gradient_list, axis=0))
```

```python
import functools
import math

import jax
import jax.numpy as jnp
from jax import lax
from jax.experimental import pallas as pl
from jax.experimental.pallas import tpu as pltpu
from jax.sharding import PartitionSpec as P

F32 = jnp.float32
BF16 = jnp.bfloat16
MESH = pl.DeviceIdType.MESH
K = 4
PLANE = 32
NT = (((1,), (1,)), ((), ()))


def split(value):
    high = value.astype(BF16)
    return high, (value - high.astype(F32)).astype(BF16)


def dot3(stacked, high, low, dims):
    rows = stacked.shape[0] // 2
    both = lax.dot_general(stacked, high, dims, preferred_element_type=F32)
    rest = lax.dot_general(stacked[:rows], low, dims, preferred_element_type=F32)
    return both[:rows] + (both[rows:] + rest)


def kernel(
    scale, psi_hbm, lam_hbm, gates_hbm, psi_out, lam_out, grad_out,
    psi_in, lam_in, gates, mats, s0, r1, s1, r2, r3, vh, vl, acc,
    psi_res, lam_res, terms, mr, yb, gout,
    in_sem, out_sem, swap_send, swap_recv, xz_send, xz_recv, y_send, y_recv, own_sem,
    rs_send, rs_recv, ye_send, ye_recv, ag_send, ag_recv,
):
    me = lax.axis_index("amp")
    y = me // PLANE
    m = lax.rem(me, PLANE)
    core = lax.rem(me, 2)
    y_high = y // 2
    y_low = lax.rem(y, 2)
    barrier = pltpu.get_barrier_semaphore()

    def remote(src, dst, send, recv, device):
        return pltpu.make_async_remote_copy(
            src_ref=src, dst_ref=dst, send_sem=send, recv_sem=recv,
            device_id=(device,), device_id_type=MESH,
        )

    def plane_peer(i):
        return lax.rem(m + i, PLANE)

    def swap_dest(j):
        return (2 * (j // 2) + 1 - y_low) * PLANE + (m - core) + j % 2

    def greet(i, carry):
        pl.semaphore_signal(
            barrier, inc=1, device_id=(y * PLANE + plane_peer(i),), device_id_type=MESH
        )
        return carry

    loads = [
        pltpu.make_async_copy(gates_hbm.at[pl.ds(0, 256)], gates.at[pl.ds(0, 256)], in_sem.at[0]),
        pltpu.make_async_copy(psi_hbm, psi_in, in_sem.at[1]),
        pltpu.make_async_copy(lam_hbm, lam_in, in_sem.at[2]),
        pltpu.make_async_copy(
            gates_hbm.at[pl.ds(256, 512)], gates.at[pl.ds(256, 512)], in_sem.at[3]
        ),
    ]
    for load in loads:
        load.start()
    lax.fori_loop(1, PLANE, greet, 0)
    for j in range(4):
        pl.semaphore_signal(barrier, inc=1, device_id=(swap_dest(j),), device_id_type=MESH)
    pl.semaphore_signal(
        barrier, inc=1, device_id=(lax.rem(y + 2, 4) * PLANE + m,), device_id_type=MESH
    )

    def build(layer):
        real_t = gates[pl.ds(layer * 256, 128), :].T
        imag_t = gates[pl.ds(layer * 256 + 128, 128), :].T
        real_high, real_low = split(real_t)
        imag_high, imag_low = split(imag_t)
        for base, real, imag in ((0, real_high, imag_high), (256, real_low, imag_low)):
            mats[layer, base:base + 128, 0:128] = real
            mats[layer, base:base + 128, 128:256] = imag
            mats[layer, base + 128:base + 256, 0:128] = -imag
            mats[layer, base + 128:base + 256, 128:256] = real

    def load_columns(read):
        for array in range(2):
            for block in range(2):
                left = (array * 2 + block) * 128
                for part in range(2):
                    high, low = split(read(array, block, part))
                    vh[part * 128:part * 128 + 128, left:left + 128] = high
                    vl[part * 128:part * 128 + 128, left:left + 128] = low

    def correlate(layer, first):
        psi_high, psi_low = vh[:, 0:256], vl[:, 0:256]
        lam_high, lam_low = vh[:, 256:512], vl[:, 256:512]
        value = (
            lax.dot_general(lam_high, psi_high, NT, preferred_element_type=F32)
            + lax.dot_general(lam_high, psi_low, NT, preferred_element_type=F32)
            + lax.dot_general(lam_low, psi_high, NT, preferred_element_type=F32)
        )
        if first:
            acc[layer] = value
        else:
            acc[layer] += value

    def apply_gate(layer):
        dims = (((1,), (0,)), ((), ()))
        return dot3(mats[layer], vh[...], vl[...], dims)

    def cut(value, array, block, part):
        left = (array * 2 + block) * 128
        return value[part * 128:part * 128 + 128, left:left + 128]

    combos = [(a, b, p) for a in range(2) for b in range(2) for p in range(2)]
    ins = (psi_in, lam_in)
    outs = (psi_res, lam_res)

    def sub(array, block, part):
        return array * 4 + block * 2 + part

    def gate0(k):
        load_columns(lambda a, b, p: ins[a][pl.ds(k * 4 + b * 2 + p, 128, stride=16), :])
        value = apply_gate(0)
        for a, b, p in combos:
            s0[k, pl.ds(sub(a, b, p), 128, stride=8), :] = cut(value, a, b, p)

    def swap_start(k):
        for j in range(4):
            remote(
                s0.at[k, pl.ds(j * 256, 256)],
                r1.at[k, pl.ds((2 * y_high + core) * 256, 256)],
                swap_send.at[k], swap_recv.at[k], swap_dest(j),
            ).start()

    def swap_wait(k):
        remote(s0.at[k], r1.at[k], swap_send.at[k], swap_recv.at[k], swap_dest(0)).wait_recv()

    def gate1(k):
        load_columns(lambda a, b, p: r1[k, pl.ds(sub(a, b, p), 128, stride=8), :])
        value = apply_gate(1)
        for a, b, p in combos:
            part = cut(value, a, b, p)
            for j in range(4):
                s1[k, pl.ds(j * 8 + sub(a, b, p), 32, stride=32), :] = part[j * 32:j * 32 + 32]

    def xz_own(k):
        return pltpu.make_async_copy(
            s1.at[k, pl.ds(m * 32, 32)], r2.at[k, pl.ds(m * 32, 32)], own_sem.at[0, k]
        )

    def xz_start(k):
        def body(i, carry):
            q = plane_peer(i)
            remote(
                s1.at[k, pl.ds(q * 32, 32)], r2.at[k, pl.ds(m * 32, 32)],
                xz_send.at[k], xz_recv.at[k], y * PLANE + q,
            ).start()
            return carry

        lax.fori_loop(1, PLANE, body, 0)
        xz_own(k).start()

    def xz_wait(k):
        remote(
            s1.at[k, pl.ds(0, 992)], r2.at[k, pl.ds(0, 992)],
            xz_send.at[k], xz_recv.at[k], swap_dest(0),
        ).wait_recv()
        xz_own(k).wait()

    r2_tiles = r2.reshape(K, 32, 4, 8, 128)
    r3_tiles = r3.reshape(K, 128, 8, 128)
    block_of_me = 2 * y_high + 1 - y_low

    def y_own(k):
        return pltpu.make_async_copy(
            r2_tiles.at[k, :, y], r3_tiles.at[k, pl.ds(block_of_me * 32, 32)], own_sem.at[1, k]
        )

    def y_start(k):
        for step in (2, 1, 3):
            to = lax.rem(y + step, 4)
            remote(
                r2_tiles.at[k, :, to], r3_tiles.at[k, pl.ds(block_of_me * 32, 32)],
                y_send.at[k], y_recv.at[k], to * PLANE + m,
            ).start()
        y_own(k).start()

    def y_wait(k):
        remote(
            r2.at[k, pl.ds(0, 768)], r3.at[k, pl.ds(0, 768)],
            y_send.at[k], y_recv.at[k], swap_dest(0),
        ).wait_recv()
        y_own(k).wait()

    def gate2_load(k):
        load_columns(lambda a, b, p: r3[k, pl.ds(sub(a, b, p), 128, stride=8), :])

    def gate2_apply(k):
        value = apply_gate(2)
        for a, b, p in combos:
            outs[a][pl.ds(k * 4 + b * 2 + p, 128, stride=16), :] = cut(value, a, b, p)

    def reduce_start(layer):
        real = acc[layer, 0:128, 0:128] + acc[layer, 128:256, 128:256]
        imag = acc[layer, 128:256, 0:128] - acc[layer, 0:128, 128:256]
        high, low = split(jnp.concatenate([real, -imag], axis=1))
        left = lax.dot_general(high, mats[layer], NT, preferred_element_type=F32)
        rest = lax.dot_general(low, mats[layer, 0:256], NT, preferred_element_type=F32)
        value = left[:, 0:256] + (left[:, 256:512] + rest)
        terms[layer, 0:128, :] = value[:, 0:128]
        terms[layer, 128:256, :] = -value[:, 128:256]
        mine = pl.ds(m * 8, 8)
        mr[layer, mine, :] = terms[layer, mine, :]

        def body(i, carry):
            q = plane_peer(i)
            remote(
                terms.at[layer, pl.ds(q * 8, 8)], mr.at[layer, mine],
                rs_send.at[layer], rs_recv.at[layer], y * PLANE + q,
            ).start()
            return carry

        lax.fori_loop(1, PLANE, body, 0)

    def reduce_middle(layer):
        remote(
            terms.at[layer, pl.ds(0, 248)], mr.at[layer, pl.ds(0, 248)],
            rs_send.at[layer], rs_recv.at[layer], swap_dest(0),
        ).wait_recv()
        total = mr[layer, 0:8, :]
        parts = [mr[layer, i * 8:i * 8 + 8, :] for i in range(PLANE)]
        while len(parts) > 1:
            parts = [parts[i] + parts[i + 1] for i in range(0, len(parts), 2)]
        total = parts[0]
        slot = pl.ds(y * 8, 8)
        yb[layer, slot, :] = total
        for step in (2, 1, 3):
            remote(
                yb.at[layer, slot], yb.at[layer, slot],
                ye_send.at[layer], ye_recv.at[layer], lax.rem(y + step, 4) * PLANE + m,
            ).start()

    def reduce_end(layer):
        remote(
            yb.at[layer, pl.ds(0, 24)], yb.at[layer, pl.ds(0, 24)],
            ye_send.at[layer], ye_recv.at[layer], swap_dest(0),
        ).wait_recv()
        total = (yb[layer, 0:8, :] + yb[layer, 8:16, :]) + (
            yb[layer, 16:24, :] + yb[layer, 24:32, :]
        )
        mine = pl.ds(m * 8, 8)
        gout[layer, mine, :] = total * scale

        def body(i, carry):
            remote(
                gout.at[layer, mine], gout.at[layer, mine],
                ag_send.at[layer], ag_recv.at[layer], y * PLANE + plane_peer(i),
            ).start()
            return carry

        lax.fori_loop(1, PLANE, body, 0)

    def reduce_wait(layer):
        remote(
            gout.at[layer, pl.ds(0, 248)], gout.at[layer, pl.ds(0, 248)],
            ag_send.at[layer], ag_recv.at[layer], swap_dest(0),
        ).wait_recv()

    loads[0].wait()
    build(0)
    loads[1].wait()
    loads[2].wait()
    for k in range(K):
        gate0(k)
        if k == 0:
            pl.semaphore_wait(barrier, PLANE - 1 + 5)
        swap_start(k)
        correlate(0, k == 0)
    loads[3].wait()
    build(1)
    reduce_start(0)
    swap_wait(0)
    gate1(0)
    xz_start(0)
    correlate(1, True)
    build(2)
    reduce_middle(0)
    swap_wait(1)
    gate1(1)
    xz_start(1)
    correlate(1, False)
    reduce_end(0)
    xz_wait(0)
    y_start(0)
    swap_wait(2)
    gate1(2)
    xz_start(2)
    correlate(1, False)
    swap_wait(3)
    gate1(3)
    xz_start(3)
    correlate(1, False)
    reduce_start(1)
    xz_wait(1)
    y_start(1)
    reduce_middle(1)
    y_wait(0)
    gate2_load(0)
    correlate(2, True)
    gate2_apply(0)
    reduce_end(1)
    xz_wait(2)
    y_start(2)
    y_wait(1)
    gate2_load(1)
    correlate(2, False)
    gate2_apply(1)
    xz_wait(3)
    y_start(3)
    y_wait(2)
    gate2_load(2)
    correlate(2, False)
    gate2_apply(2)
    y_wait(3)
    gate2_load(3)
    correlate(2, False)
    reduce_start(2)
    gate2_apply(3)
    stores = [
        pltpu.make_async_copy(psi_res, psi_out, out_sem.at[0]),
        pltpu.make_async_copy(lam_res, lam_out, out_sem.at[1]),
    ]
    for store in stores:
        store.start()
    reduce_middle(2)
    reduce_wait(0)
    reduce_wait(1)
    reduce_end(2)
    reduce_wait(2)
    grad_store = pltpu.make_async_copy(gout, grad_out, out_sem.at[2])
    grad_store.start()

    for k in range(K):
        remote(s0.at[k], r1.at[k], swap_send.at[k], swap_recv.at[k], swap_dest(0)).wait_send()
        remote(
            s1.at[k, pl.ds(0, 992)], r2.at[k, pl.ds(0, 992)],
            xz_send.at[k], xz_recv.at[k], swap_dest(0),
        ).wait_send()
        remote(
            r2.at[k, pl.ds(0, 768)], r3.at[k, pl.ds(0, 768)],
            y_send.at[k], y_recv.at[k], swap_dest(0),
        ).wait_send()
    for layer in range(3):
        remote(
            terms.at[layer, pl.ds(0, 248)], mr.at[layer, pl.ds(0, 248)],
            rs_send.at[layer], rs_recv.at[layer], swap_dest(0),
        ).wait_send()
        remote(
            yb.at[layer, pl.ds(0, 24)], yb.at[layer, pl.ds(0, 24)],
            ye_send.at[layer], ye_recv.at[layer], swap_dest(0),
        ).wait_send()
        remote(
            gout.at[layer, pl.ds(0, 248)], gout.at[layer, pl.ds(0, 248)],
            ag_send.at[layer], ag_recv.at[layer], swap_dest(0),
        ).wait_send()
    for store in stores:
        store.wait()
    grad_store.wait()


def rows_of(field):
    return field.reshape(2, 1024, 128).transpose(1, 0, 2).reshape(2048, 128)


def field_of(rows):
    return rows.reshape(1024, 2, 128).transpose(1, 0, 2).reshape(2, 131072)


def on_device(state, costate, gates):
    scale = 1.0 / math.sqrt(128 * 1024)
    dma = pltpu.SemaphoreType.DMA
    psi, lam, grads = pl.pallas_call(
        functools.partial(kernel, scale),
        out_shape=(
            jax.ShapeDtypeStruct((2048, 128), F32),
            jax.ShapeDtypeStruct((2048, 128), F32),
            jax.ShapeDtypeStruct((3, 256, 128), F32),
        ),
        in_specs=[pl.BlockSpec(memory_space=pl.ANY)] * 3,
        out_specs=[pl.BlockSpec(memory_space=pl.ANY)] * 3,
        scratch_shapes=[
            pltpu.VMEM((2048, 128), F32),
            pltpu.VMEM((2048, 128), F32),
            pltpu.VMEM((768, 128), F32),
            pltpu.VMEM((3, 512, 256), BF16),
            pltpu.VMEM((K, 1024, 128), F32),
            pltpu.VMEM((K, 1024, 128), F32),
            pltpu.VMEM((K, 1024, 128), F32),
            pltpu.VMEM((K, 1024, 128), F32),
            pltpu.VMEM((K, 1024, 128), F32),
            pltpu.VMEM((256, 512), BF16),
            pltpu.VMEM((256, 512), BF16),
            pltpu.VMEM((3, 256, 256), F32),
            pltpu.VMEM((2048, 128), F32),
            pltpu.VMEM((2048, 128), F32),
            pltpu.VMEM((3, 256, 128), F32),
            pltpu.VMEM((3, 256, 128), F32),
            pltpu.VMEM((3, 32, 128), F32),
            pltpu.VMEM((3, 256, 128), F32),
            dma((4,)), dma((3,)),
            dma((K,)), dma((K,)), dma((K,)), dma((K,)), dma((K,)), dma((K,)), dma((2, K)),
            dma((3,)), dma((3,)), dma((3,)), dma((3,)), dma((3,)), dma((3,)),
        ],
        compiler_params=pltpu.CompilerParams(collective_id=0, has_side_effects=True),
        name="window",
    )(rows_of(state), rows_of(costate), gates.reshape(768, 128))
    return field_of(psi), field_of(lam), grads.reshape(3, 2, 128, 128)


def solution(mesh):
    return jax.shard_map(
        on_device,
        mesh=mesh,
        in_specs=(P(None, "amp"), P(None, "amp"), P()),
        out_specs=(P(None, "amp"), P(None, "amp"), P()),
        check_vma=False,
    )
```

```python
import functools
import math

import jax
import jax.numpy as jnp
from jax import lax
from jax.experimental import pallas as pl
from jax.experimental.pallas import tpu as pltpu
from jax.sharding import PartitionSpec as P

F32 = jnp.float32
BF16 = jnp.bfloat16
MESH = pl.DeviceIdType.MESH
K = 4
PLANE = 32
NT = (((1,), (1,)), ((), ()))


def split(value):
    high = value.astype(BF16)
    return high, (value - high.astype(F32)).astype(BF16)


def dot3(stacked, high, low, dims):
    rows = stacked.shape[0] // 2
    both = lax.dot_general(stacked, high, dims, preferred_element_type=F32)
    rest = lax.dot_general(stacked[:rows], low, dims, preferred_element_type=F32)
    return both[:rows] + (both[rows:] + rest)


def kernel(
    scale, psi_hbm, lam_hbm, gates_hbm, psi_out, lam_out, grad_out,
    psi_in, lam_in, gates, mats, s0, r1, s1, r2, r3, vh, vl, acc,
    psi_res, lam_res, terms, mr, yb, gout,
    in_sem, out_sem, swap_send, swap_recv, xz_send, xz_recv, y_send, y_recv, own_sem,
    rs_send, rs_recv, ye_send, ye_recv, ag_send, ag_recv,
):
    me = lax.axis_index("amp")
    y = me // PLANE
    m = lax.rem(me, PLANE)
    core = lax.rem(me, 2)
    y_high = y // 2
    y_low = lax.rem(y, 2)
    barrier = pltpu.get_barrier_semaphore()

    def remote(src, dst, send, recv, device):
        return pltpu.make_async_remote_copy(
            src_ref=src, dst_ref=dst, send_sem=send, recv_sem=recv,
            device_id=(device,), device_id_type=MESH,
        )

    def plane_peer(i):
        return lax.rem(m + i, PLANE)

    def swap_dest(j):
        return (2 * (j // 2) + 1 - y_low) * PLANE + (m - core) + j % 2

    def greet(i, carry):
        pl.semaphore_signal(
            barrier, inc=1, device_id=(y * PLANE + plane_peer(i),), device_id_type=MESH
        )
        return carry

    loads = [
        pltpu.make_async_copy(gates_hbm.at[pl.ds(0, 256)], gates.at[pl.ds(0, 256)], in_sem.at[0]),
        pltpu.make_async_copy(psi_hbm, psi_in, in_sem.at[1]),
        pltpu.make_async_copy(lam_hbm, lam_in, in_sem.at[2]),
        pltpu.make_async_copy(
            gates_hbm.at[pl.ds(256, 512)], gates.at[pl.ds(256, 512)], in_sem.at[3]
        ),
    ]
    for load in loads:
        load.start()
    lax.fori_loop(1, PLANE, greet, 0)
    for j in range(4):
        pl.semaphore_signal(barrier, inc=1, device_id=(swap_dest(j),), device_id_type=MESH)
    pl.semaphore_signal(
        barrier, inc=1, device_id=(lax.rem(y + 2, 4) * PLANE + m,), device_id_type=MESH
    )

    def build(layer):
        real_t = gates[pl.ds(layer * 256, 128), :].T
        imag_t = gates[pl.ds(layer * 256 + 128, 128), :].T
        real_high, real_low = split(real_t)
        imag_high, imag_low = split(imag_t)
        for base, real, imag in ((0, real_high, imag_high), (256, real_low, imag_low)):
            mats[layer, base:base + 128, 0:128] = real
            mats[layer, base:base + 128, 128:256] = imag
            mats[layer, base + 128:base + 256, 0:128] = -imag
            mats[layer, base + 128:base + 256, 128:256] = real

    def load_columns(read):
        for array in range(2):
            for block in range(2):
                left = (array * 2 + block) * 128
                for part in range(2):
                    high, low = split(read(array, block, part))
                    vh[part * 128:part * 128 + 128, left:left + 128] = high
                    vl[part * 128:part * 128 + 128, left:left + 128] = low

    def correlate(layer, first):
        psi_high, psi_low = vh[:, 0:256], vl[:, 0:256]
        lam_high, lam_low = vh[:, 256:512], vl[:, 256:512]
        value = (
            lax.dot_general(lam_high, psi_high, NT, preferred_element_type=F32)
            + lax.dot_general(lam_high, psi_low, NT, preferred_element_type=F32)
            + lax.dot_general(lam_low, psi_high, NT, preferred_element_type=F32)
        )
        if first:
            acc[layer] = value
        else:
            acc[layer] += value

    def apply_gate(layer):
        dims = (((1,), (0,)), ((), ()))
        return dot3(mats[layer], vh[...], vl[...], dims)

    def cut(value, array, block, part):
        left = (array * 2 + block) * 128
        return value[part * 128:part * 128 + 128, left:left + 128]

    combos = [(a, b, p) for a in range(2) for b in range(2) for p in range(2)]
    ins = (psi_in, lam_in)
    outs = (psi_res, lam_res)

    def sub(array, block, part):
        return array * 4 + block * 2 + part

    def gate0(k):
        load_columns(lambda a, b, p: ins[a][pl.ds(k * 4 + b * 2 + p, 128, stride=16), :])
        value = apply_gate(0)
        for a, b, p in combos:
            s0[k, pl.ds(sub(a, b, p), 128, stride=8), :] = cut(value, a, b, p)

    def swap_start(k):
        for j in range(4):
            remote(
                s0.at[k, pl.ds(j * 256, 256)],
                r1.at[k, pl.ds((2 * y_high + core) * 256, 256)],
                swap_send.at[k], swap_recv.at[k], swap_dest(j),
            ).start()

    def swap_wait(k):
        remote(s0.at[k], r1.at[k], swap_send.at[k], swap_recv.at[k], swap_dest(0)).wait_recv()

    def gate1(k):
        load_columns(lambda a, b, p: r1[k, pl.ds(sub(a, b, p), 128, stride=8), :])
        value = apply_gate(1)
        for a, b, p in combos:
            part = cut(value, a, b, p)
            for j in range(4):
                s1[k, pl.ds(j * 8 + sub(a, b, p), 32, stride=32), :] = part[j * 32:j * 32 + 32]

    def xz_own(k):
        return pltpu.make_async_copy(
            s1.at[k, pl.ds(m * 32, 32)], r2.at[k, pl.ds(m * 32, 32)], own_sem.at[0, k]
        )

    def xz_start(k):
        def body(i, carry):
            q = plane_peer(i)
            remote(
                s1.at[k, pl.ds(q * 32, 32)], r2.at[k, pl.ds(m * 32, 32)],
                xz_send.at[k], xz_recv.at[k], y * PLANE + q,
            ).start()
            return carry

        lax.fori_loop(1, PLANE, body, 0)
        xz_own(k).start()

    def xz_wait(k):
        remote(
            s1.at[k, pl.ds(0, 992)], r2.at[k, pl.ds(0, 992)],
            xz_send.at[k], xz_recv.at[k], swap_dest(0),
        ).wait_recv()
        xz_own(k).wait()

    r2_tiles = r2.reshape(K, 32, 4, 8, 128)
    r3_tiles = r3.reshape(K, 128, 8, 128)
    block_of_me = 2 * y_high + 1 - y_low

    def y_own(k):
        return pltpu.make_async_copy(
            r2_tiles.at[k, :, y], r3_tiles.at[k, pl.ds(block_of_me * 32, 32)], own_sem.at[1, k]
        )

    def y_start(k):
        for step in (2, 1, 3):
            to = lax.rem(y + step, 4)
            remote(
                r2_tiles.at[k, :, to], r3_tiles.at[k, pl.ds(block_of_me * 32, 32)],
                y_send.at[k], y_recv.at[k], to * PLANE + m,
            ).start()
        y_own(k).start()

    def y_wait(k):
        remote(
            r2.at[k, pl.ds(0, 768)], r3.at[k, pl.ds(0, 768)],
            y_send.at[k], y_recv.at[k], swap_dest(0),
        ).wait_recv()
        y_own(k).wait()

    def gate2_load(k):
        load_columns(lambda a, b, p: r3[k, pl.ds(sub(a, b, p), 128, stride=8), :])

    def gate2_apply(k):
        value = apply_gate(2)
        for a, b, p in combos:
            outs[a][pl.ds(k * 4 + b * 2 + p, 128, stride=16), :] = cut(value, a, b, p)

    def reduce_start(layer):
        real = acc[layer, 0:128, 0:128] + acc[layer, 128:256, 128:256]
        imag = acc[layer, 128:256, 0:128] - acc[layer, 0:128, 128:256]
        high, low = split(jnp.concatenate([real, -imag], axis=1))
        left = lax.dot_general(high, mats[layer], NT, preferred_element_type=F32)
        rest = lax.dot_general(low, mats[layer, 0:256], NT, preferred_element_type=F32)
        value = left[:, 0:256] + (left[:, 256:512] + rest)
        terms[layer, 0:128, :] = value[:, 0:128]
        terms[layer, 128:256, :] = -value[:, 128:256]
        mine = pl.ds(m * 8, 8)
        mr[layer, mine, :] = terms[layer, mine, :]

        def body(i, carry):
            q = plane_peer(i)
            remote(
                terms.at[layer, pl.ds(q * 8, 8)], mr.at[layer, mine],
                rs_send.at[layer], rs_recv.at[layer], y * PLANE + q,
            ).start()
            return carry

        lax.fori_loop(1, PLANE, body, 0)

    def reduce_middle(layer):
        remote(
            terms.at[layer, pl.ds(0, 248)], mr.at[layer, pl.ds(0, 248)],
            rs_send.at[layer], rs_recv.at[layer], swap_dest(0),
        ).wait_recv()
        total = mr[layer, 0:8, :]
        parts = [mr[layer, i * 8:i * 8 + 8, :] for i in range(PLANE)]
        while len(parts) > 1:
            parts = [parts[i] + parts[i + 1] for i in range(0, len(parts), 2)]
        total = parts[0]
        slot = pl.ds(y * 8, 8)
        yb[layer, slot, :] = total
        for step in (2, 1, 3):
            remote(
                yb.at[layer, slot], yb.at[layer, slot],
                ye_send.at[layer], ye_recv.at[layer], lax.rem(y + step, 4) * PLANE + m,
            ).start()

    def reduce_end(layer):
        remote(
            yb.at[layer, pl.ds(0, 24)], yb.at[layer, pl.ds(0, 24)],
            ye_send.at[layer], ye_recv.at[layer], swap_dest(0),
        ).wait_recv()
        total = (yb[layer, 0:8, :] + yb[layer, 8:16, :]) + (
            yb[layer, 16:24, :] + yb[layer, 24:32, :]
        )
        mine = pl.ds(m * 8, 8)
        gout[layer, mine, :] = total * scale

        def body(i, carry):
            remote(
                gout.at[layer, mine], gout.at[layer, mine],
                ag_send.at[layer], ag_recv.at[layer], y * PLANE + plane_peer(i),
            ).start()
            return carry

        lax.fori_loop(1, PLANE, body, 0)

    def reduce_wait(layer):
        remote(
            gout.at[layer, pl.ds(0, 248)], gout.at[layer, pl.ds(0, 248)],
            ag_send.at[layer], ag_recv.at[layer], swap_dest(0),
        ).wait_recv()

    loads[0].wait()
    build(0)
    loads[1].wait()
    loads[2].wait()
    for k in range(K):
        gate0(k)
        if k == 0:
            pl.semaphore_wait(barrier, PLANE - 1 + 5)
        swap_start(k)
        correlate(0, k == 0)
    loads[3].wait()
    build(1)
    reduce_start(0)
    swap_wait(0)
    gate1(0)
    xz_start(0)
    correlate(1, True)
    build(2)
    swap_wait(1)
    gate1(1)
    xz_start(1)
    correlate(1, False)
    reduce_middle(0)
    xz_wait(0)
    y_start(0)
    swap_wait(2)
    gate1(2)
    xz_start(2)
    correlate(1, False)
    swap_wait(3)
    gate1(3)
    xz_start(3)
    correlate(1, False)
    reduce_start(1)
    xz_wait(1)
    y_start(1)
    y_wait(0)
    gate2_load(0)
    correlate(2, True)
    gate2_apply(0)
    reduce_end(0)
    xz_wait(2)
    y_start(2)
    reduce_middle(1)
    xz_wait(3)
    y_start(3)
    y_wait(1)
    gate2_load(1)
    correlate(2, False)
    gate2_apply(1)
    y_wait(2)
    gate2_load(2)
    correlate(2, False)
    gate2_apply(2)
    reduce_end(1)
    y_wait(3)
    gate2_load(3)
    correlate(2, False)
    reduce_start(2)
    gate2_apply(3)
    stores = [
        pltpu.make_async_copy(psi_res, psi_out, out_sem.at[0]),
        pltpu.make_async_copy(lam_res, lam_out, out_sem.at[1]),
    ]
    for store in stores:
        store.start()
    reduce_middle(2)
    reduce_wait(0)
    reduce_wait(1)
    reduce_end(2)
    reduce_wait(2)
    grad_store = pltpu.make_async_copy(gout, grad_out, out_sem.at[2])
    grad_store.start()

    for k in range(K):
        remote(s0.at[k], r1.at[k], swap_send.at[k], swap_recv.at[k], swap_dest(0)).wait_send()
        remote(
            s1.at[k, pl.ds(0, 992)], r2.at[k, pl.ds(0, 992)],
            xz_send.at[k], xz_recv.at[k], swap_dest(0),
        ).wait_send()
        remote(
            r2.at[k, pl.ds(0, 768)], r3.at[k, pl.ds(0, 768)],
            y_send.at[k], y_recv.at[k], swap_dest(0),
        ).wait_send()
    for layer in range(3):
        remote(
            terms.at[layer, pl.ds(0, 248)], mr.at[layer, pl.ds(0, 248)],
            rs_send.at[layer], rs_recv.at[layer], swap_dest(0),
        ).wait_send()
        remote(
            yb.at[layer, pl.ds(0, 24)], yb.at[layer, pl.ds(0, 24)],
            ye_send.at[layer], ye_recv.at[layer], swap_dest(0),
        ).wait_send()
        remote(
            gout.at[layer, pl.ds(0, 248)], gout.at[layer, pl.ds(0, 248)],
            ag_send.at[layer], ag_recv.at[layer], swap_dest(0),
        ).wait_send()
    for store in stores:
        store.wait()
    grad_store.wait()


def rows_of(field):
    return field.reshape(2, 1024, 128).transpose(1, 0, 2).reshape(2048, 128)


def field_of(rows):
    return rows.reshape(1024, 2, 128).transpose(1, 0, 2).reshape(2, 131072)


def on_device(state, costate, gates):
    scale = 1.0 / math.sqrt(128 * 1024)
    dma = pltpu.SemaphoreType.DMA
    psi, lam, grads = pl.pallas_call(
        functools.partial(kernel, scale),
        out_shape=(
            jax.ShapeDtypeStruct((2048, 128), F32),
            jax.ShapeDtypeStruct((2048, 128), F32),
            jax.ShapeDtypeStruct((3, 256, 128), F32),
        ),
        in_specs=[pl.BlockSpec(memory_space=pl.ANY)] * 3,
        out_specs=[pl.BlockSpec(memory_space=pl.ANY)] * 3,
        scratch_shapes=[
            pltpu.VMEM((2048, 128), F32),
            pltpu.VMEM((2048, 128), F32),
            pltpu.VMEM((768, 128), F32),
            pltpu.VMEM((3, 512, 256), BF16),
            pltpu.VMEM((K, 1024, 128), F32),
            pltpu.VMEM((K, 1024, 128), F32),
            pltpu.VMEM((K, 1024, 128), F32),
            pltpu.VMEM((K, 1024, 128), F32),
            pltpu.VMEM((K, 1024, 128), F32),
            pltpu.VMEM((256, 512), BF16),
            pltpu.VMEM((256, 512), BF16),
            pltpu.VMEM((3, 256, 256), F32),
            pltpu.VMEM((2048, 128), F32),
            pltpu.VMEM((2048, 128), F32),
            pltpu.VMEM((3, 256, 128), F32),
            pltpu.VMEM((3, 256, 128), F32),
            pltpu.VMEM((3, 32, 128), F32),
            pltpu.VMEM((3, 256, 128), F32),
            dma((4,)), dma((3,)),
            dma((K,)), dma((K,)), dma((K,)), dma((K,)), dma((K,)), dma((K,)), dma((2, K)),
            dma((3,)), dma((3,)), dma((3,)), dma((3,)), dma((3,)), dma((3,)),
        ],
        compiler_params=pltpu.CompilerParams(collective_id=0, has_side_effects=True),
        name="window",
    )(rows_of(state), rows_of(costate), gates.reshape(768, 128))
    return field_of(psi), field_of(lam), grads.reshape(3, 2, 128, 128)


def solution(mesh):
    return jax.shard_map(
        on_device,
        mesh=mesh,
        in_specs=(P(None, "amp"), P(None, "amp"), P()),
        out_specs=(P(None, "amp"), P(None, "amp"), P()),
        check_vma=False,
    )
```

```python
import functools
import math

import jax
import jax.numpy as jnp
from jax import lax
from jax.experimental import pallas as pl
from jax.experimental.pallas import tpu as pltpu
from jax.sharding import PartitionSpec as P

F32 = jnp.float32
BF16 = jnp.bfloat16
MESH = pl.DeviceIdType.MESH
K = 4
PLANE = 32
NT = (((1,), (1,)), ((), ()))


def split(value):
    high = value.astype(BF16)
    return high, (value - high.astype(F32)).astype(BF16)


def dot3(stacked, high, low, dims):
    rows = stacked.shape[0] // 2
    both = lax.dot_general(stacked, high, dims, preferred_element_type=F32)
    rest = lax.dot_general(stacked[:rows], low, dims, preferred_element_type=F32)
    return both[:rows] + (both[rows:] + rest)


def kernel(
    scale, psi_hbm, lam_hbm, gates_hbm, psi_res, lam_res, gout,
    psi_in, lam_in, gates, mats, s0, r1, s1, r2, r3, vh, vl, acc,
    terms, mr, yb,
    in_sem, entry_sem, swap_send, swap_recv, xz_send, xz_recv, y_send, y_recv, own_sem,
    rs_send, rs_recv, ye_send, ye_recv, ag_send, ag_recv,
):
    me = lax.axis_index("amp")
    y = me // PLANE
    m = lax.rem(me, PLANE)
    core = lax.rem(me, 2)
    y_high = y // 2
    y_low = lax.rem(y, 2)
    barrier = pltpu.get_barrier_semaphore()

    def remote(src, dst, send, recv, device):
        return pltpu.make_async_remote_copy(
            src_ref=src, dst_ref=dst, send_sem=send, recv_sem=recv,
            device_id=(device,), device_id_type=MESH,
        )

    x, z = m // 8, lax.rem(m // 2, 4)

    def peer(dx, dz, other):
        return lax.rem(x + dx, 4) * 8 + lax.rem(z + dz, 4) * 2 + lax.rem(core + other, 2)

    def at(dy, dx, dz, other):
        return lax.rem(y + dy, 4) * PLANE + peer(dx, dz, other)

    hops = (0, 1, 2, 1)
    offsets = [(dx, dz, o) for dx in range(4) for dz in range(4) for o in range(2)]
    offsets = sorted(offsets, key=lambda d: -(hops[d[0]] + hops[d[1]]))[:-2] + [(0, 0, 1)]

    def swap_dest(j):
        return (2 * (j // 2) + 1 - y_low) * PLANE + (m - core) + j % 2

    near = [(dy, 0, 0, o) for dy in (1, 3) for o in range(2)]
    near += [(0, dx, 0, o) for dx in (1, 3) for o in range(2)]
    near += [(0, 0, dz, o) for dz in (1, 3) for o in range(2)] + [(0, 0, 0, 1)]
    rounds = (
        [(dy, 0, 0, 0) for dy in (1, 3)] + [(0, dx, 0, 0) for dx in (1, 3)],
        [(0, 0, dz, 0) for dz in (1, 3)],
        [(0, 0, dz, 0) for dz in (1, 3)],
    )

    def tell(semaphore, where):
        for offset in where:
            pl.semaphore_signal(
                semaphore, inc=1, device_id=(at(*offset),), device_id_type=MESH
            )

    loads = [
        pltpu.make_async_copy(gates_hbm.at[pl.ds(0, 256)], gates.at[pl.ds(0, 256)], in_sem.at[0]),
        pltpu.make_async_copy(psi_hbm, psi_in, in_sem.at[1]),
        pltpu.make_async_copy(lam_hbm, lam_in, in_sem.at[2]),
        pltpu.make_async_copy(
            gates_hbm.at[pl.ds(256, 512)], gates.at[pl.ds(256, 512)], in_sem.at[3]
        ),
    ]
    for load in loads:
        load.start()
    tell(barrier, near)

    def build(layer):
        real_t = gates[pl.ds(layer * 256, 128), :].T
        imag_t = gates[pl.ds(layer * 256 + 128, 128), :].T
        real_high, real_low = split(real_t)
        imag_high, imag_low = split(imag_t)
        for base, real, imag in ((0, real_high, imag_high), (256, real_low, imag_low)):
            mats[layer, base:base + 128, 0:128] = real
            mats[layer, base:base + 128, 128:256] = imag
            mats[layer, base + 128:base + 256, 0:128] = -imag
            mats[layer, base + 128:base + 256, 128:256] = real

    def load_columns(read):
        for array in range(2):
            for block in range(2):
                left = (array * 2 + block) * 128
                for part in range(2):
                    high, low = split(read(array, block, part))
                    vh[part * 128:part * 128 + 128, left:left + 128] = high
                    vl[part * 128:part * 128 + 128, left:left + 128] = low

    def correlate(layer, first):
        psi_high, psi_low = vh[:, 0:256], vl[:, 0:256]
        lam_high, lam_low = vh[:, 256:512], vl[:, 256:512]
        value = (
            lax.dot_general(lam_high, psi_high, NT, preferred_element_type=F32)
            + lax.dot_general(lam_high, psi_low, NT, preferred_element_type=F32)
            + lax.dot_general(lam_low, psi_high, NT, preferred_element_type=F32)
        )
        if first:
            acc[layer] = value
        else:
            acc[layer] += value

    def apply_gate(layer):
        dims = (((1,), (0,)), ((), ()))
        return dot3(mats[layer], vh[...], vl[...], dims)

    def cut(value, array, block, part):
        left = (array * 2 + block) * 128
        return value[part * 128:part * 128 + 128, left:left + 128]

    combos = [(a, b, p) for a in range(2) for b in range(2) for p in range(2)]
    ins = (psi_in, lam_in)
    outs = (psi_res, lam_res)

    def sub(array, block, part):
        return array * 4 + block * 2 + part

    def gate0(k):
        load_columns(lambda a, b, p: ins[a][pl.ds(k * 4 + b * 2 + p, 128, stride=16), :])
        value = apply_gate(0)
        for a, b, p in combos:
            s0[k, pl.ds(sub(a, b, p), 128, stride=8), :] = cut(value, a, b, p)

    def swap_start(k):
        for j in range(4):
            remote(
                s0.at[k, pl.ds(j * 256, 256)],
                r1.at[k, pl.ds((2 * y_high + core) * 256, 256)],
                swap_send.at[k], swap_recv.at[k], swap_dest(j),
            ).start()

    def swap_wait(k):
        remote(s0.at[k], r1.at[k], swap_send.at[k], swap_recv.at[k], swap_dest(0)).wait_recv()

    def gate1(k):
        load_columns(lambda a, b, p: r1[k, pl.ds(sub(a, b, p), 128, stride=8), :])
        value = apply_gate(1)
        for a, b, p in combos:
            part = cut(value, a, b, p)
            for j in range(4):
                s1[k, pl.ds(j * 8 + sub(a, b, p), 32, stride=32), :] = part[j * 32:j * 32 + 32]

    def xz_own(k):
        return pltpu.make_async_copy(
            s1.at[k, pl.ds(m * 32, 32)], r2.at[k, pl.ds(m * 32, 32)], own_sem.at[0, k]
        )

    def xz_start(k):
        for offset in offsets:
            q = peer(*offset)
            remote(
                s1.at[k, pl.ds(q * 32, 32)], r2.at[k, pl.ds(m * 32, 32)],
                xz_send.at[k], xz_recv.at[k], y * PLANE + q,
            ).start()
        xz_own(k).start()

    def xz_wait(k):
        remote(
            s1.at[k, pl.ds(0, 992)], r2.at[k, pl.ds(0, 992)],
            xz_send.at[k], xz_recv.at[k], swap_dest(0),
        ).wait_recv()
        xz_own(k).wait()

    r2_tiles = r2.reshape(K, 32, 4, 8, 128)
    r3_tiles = r3.reshape(K, 128, 8, 128)
    block_of_me = 2 * y_high + 1 - y_low

    def y_own(k):
        return pltpu.make_async_copy(
            r2_tiles.at[k, :, y], r3_tiles.at[k, pl.ds(block_of_me * 32, 32)], own_sem.at[1, k]
        )

    def y_start(k):
        for step in (2, 1, 3):
            to = lax.rem(y + step, 4)
            remote(
                r2_tiles.at[k, :, to], r3_tiles.at[k, pl.ds(block_of_me * 32, 32)],
                y_send.at[k], y_recv.at[k], to * PLANE + m,
            ).start()
        y_own(k).start()

    def y_wait(k):
        remote(
            r2.at[k, pl.ds(0, 768)], r3.at[k, pl.ds(0, 768)],
            y_send.at[k], y_recv.at[k], swap_dest(0),
        ).wait_recv()
        y_own(k).wait()

    def gate2_load(k):
        load_columns(lambda a, b, p: r3[k, pl.ds(sub(a, b, p), 128, stride=8), :])

    def gate2_apply(k):
        value = apply_gate(2)
        for a, b, p in combos:
            outs[a][pl.ds(k * 4 + b * 2 + p, 128, stride=16), :] = cut(value, a, b, p)

    def reduce_start(layer):
        real = acc[layer, 0:128, 0:128] + acc[layer, 128:256, 128:256]
        imag = acc[layer, 128:256, 0:128] - acc[layer, 0:128, 128:256]
        high, low = split(jnp.concatenate([real, -imag], axis=1))
        left = lax.dot_general(high, mats[layer], NT, preferred_element_type=F32)
        rest = lax.dot_general(low, mats[layer, 0:256], NT, preferred_element_type=F32)
        value = left[:, 0:256] + (left[:, 256:512] + rest)
        terms[layer, 0:128, :] = value[:, 0:128]
        terms[layer, 128:256, :] = -value[:, 128:256]
        mine = pl.ds(m * 8, 8)
        mr[layer, mine, :] = terms[layer, mine, :]

        for offset in offsets:
            q = peer(*offset)
            remote(
                terms.at[layer, pl.ds(q * 8, 8)], mr.at[layer, mine],
                rs_send.at[layer], rs_recv.at[layer], y * PLANE + q,
            ).start()

    def reduce_middle(layer):
        remote(
            terms.at[layer, pl.ds(0, 248)], mr.at[layer, pl.ds(0, 248)],
            rs_send.at[layer], rs_recv.at[layer], swap_dest(0),
        ).wait_recv()
        total = mr[layer, 0:8, :]
        parts = [mr[layer, i * 8:i * 8 + 8, :] for i in range(PLANE)]
        while len(parts) > 1:
            parts = [parts[i] + parts[i + 1] for i in range(0, len(parts), 2)]
        total = parts[0]
        slot = pl.ds(y * 8, 8)
        yb[layer, slot, :] = total
        for step in (2, 1, 3):
            remote(
                yb.at[layer, slot], yb.at[layer, slot],
                ye_send.at[layer], ye_recv.at[layer], lax.rem(y + step, 4) * PLANE + m,
            ).start()

    def reduce_end(layer):
        remote(
            yb.at[layer, pl.ds(0, 24)], yb.at[layer, pl.ds(0, 24)],
            ye_send.at[layer], ye_recv.at[layer], swap_dest(0),
        ).wait_recv()
        total = (yb[layer, 0:8, :] + yb[layer, 8:16, :]) + (
            yb[layer, 16:24, :] + yb[layer, 24:32, :]
        )
        mine = pl.ds(m * 8, 8)
        gout[layer, mine, :] = total * scale

        for offset in offsets:
            remote(
                gout.at[layer, mine], gout.at[layer, mine],
                ag_send.at[layer], ag_recv.at[layer], y * PLANE + peer(*offset),
            ).start()

    def reduce_wait(layer):
        remote(
            gout.at[layer, pl.ds(0, 248)], gout.at[layer, pl.ds(0, 248)],
            ag_send.at[layer], ag_recv.at[layer], swap_dest(0),
        ).wait_recv()

    loads[0].wait()
    build(0)
    loads[1].wait()
    loads[2].wait()
    for k in range(K):
        gate0(k)
        if k == 0:
            pl.semaphore_wait(barrier, len(near))
        else:
            pl.semaphore_wait(entry_sem.at[k - 1], len(rounds[k - 1]))
        if k < 3:
            tell(entry_sem.at[k], rounds[k])
        swap_start(k)
        correlate(0, k == 0)
    loads[3].wait()
    build(1)
    reduce_start(0)
    swap_wait(0)
    gate1(0)
    xz_start(0)
    correlate(1, True)
    build(2)
    swap_wait(1)
    gate1(1)
    xz_start(1)
    correlate(1, False)
    reduce_middle(0)
    xz_wait(0)
    y_start(0)
    swap_wait(2)
    gate1(2)
    xz_start(2)
    correlate(1, False)
    swap_wait(3)
    gate1(3)
    xz_start(3)
    correlate(1, False)
    reduce_start(1)
    xz_wait(1)
    y_start(1)
    y_wait(0)
    gate2_load(0)
    correlate(2, True)
    gate2_apply(0)
    reduce_end(0)
    xz_wait(2)
    y_start(2)
    reduce_middle(1)
    xz_wait(3)
    y_start(3)
    y_wait(1)
    gate2_load(1)
    correlate(2, False)
    gate2_apply(1)
    y_wait(2)
    gate2_load(2)
    correlate(2, False)
    gate2_apply(2)
    reduce_end(1)
    y_wait(3)
    gate2_load(3)
    correlate(2, False)
    reduce_start(2)
    gate2_apply(3)
    reduce_middle(2)
    reduce_wait(0)
    reduce_wait(1)
    reduce_end(2)
    reduce_wait(2)

    for k in range(K):
        remote(s0.at[k], r1.at[k], swap_send.at[k], swap_recv.at[k], swap_dest(0)).wait_send()
        remote(
            s1.at[k, pl.ds(0, 992)], r2.at[k, pl.ds(0, 992)],
            xz_send.at[k], xz_recv.at[k], swap_dest(0),
        ).wait_send()
        remote(
            r2.at[k, pl.ds(0, 768)], r3.at[k, pl.ds(0, 768)],
            y_send.at[k], y_recv.at[k], swap_dest(0),
        ).wait_send()
    for layer in range(3):
        remote(
            terms.at[layer, pl.ds(0, 248)], mr.at[layer, pl.ds(0, 248)],
            rs_send.at[layer], rs_recv.at[layer], swap_dest(0),
        ).wait_send()
        remote(
            yb.at[layer, pl.ds(0, 24)], yb.at[layer, pl.ds(0, 24)],
            ye_send.at[layer], ye_recv.at[layer], swap_dest(0),
        ).wait_send()
        remote(
            gout.at[layer, pl.ds(0, 248)], gout.at[layer, pl.ds(0, 248)],
            ag_send.at[layer], ag_recv.at[layer], swap_dest(0),
        ).wait_send()


def store_kernel(psi_res, lam_res, gout, psi_out, lam_out, grad_out, sem):
    copies = [
        pltpu.make_async_copy(src, dst, sem.at[i])
        for i, (src, dst) in enumerate(((psi_res, psi_out), (lam_res, lam_out), (gout, grad_out)))
    ]
    for copy in copies:
        copy.start()
    for copy in copies:
        copy.wait()


def rows_of(field):
    return field.reshape(2, 1024, 128).transpose(1, 0, 2).reshape(2048, 128)


def field_of(rows):
    return rows.reshape(1024, 2, 128).transpose(1, 0, 2).reshape(2, 131072)


def on_device(state, costate, gates):
    scale = 1.0 / math.sqrt(128 * 1024)
    dma = pltpu.SemaphoreType.DMA
    shapes = ((2048, 128), (2048, 128), (3, 256, 128))
    results = pl.pallas_call(
        functools.partial(kernel, scale),
        out_shape=tuple(pltpu.VMEM(shape, F32) for shape in shapes),
        in_specs=[pl.BlockSpec(memory_space=pl.ANY)] * 3,
        out_specs=[pl.BlockSpec(memory_space=pltpu.VMEM)] * 3,
        scratch_shapes=[
            pltpu.VMEM((2048, 128), F32),
            pltpu.VMEM((2048, 128), F32),
            pltpu.VMEM((768, 128), F32),
            pltpu.VMEM((3, 512, 256), BF16),
            pltpu.VMEM((K, 1024, 128), F32),
            pltpu.VMEM((K, 1024, 128), F32),
            pltpu.VMEM((K, 1024, 128), F32),
            pltpu.VMEM((K, 1024, 128), F32),
            pltpu.VMEM((K, 1024, 128), F32),
            pltpu.VMEM((256, 512), BF16),
            pltpu.VMEM((256, 512), BF16),
            pltpu.VMEM((3, 256, 256), F32),
            pltpu.VMEM((3, 256, 128), F32),
            pltpu.VMEM((3, 256, 128), F32),
            pltpu.VMEM((3, 32, 128), F32),
            dma((4,)), pltpu.SemaphoreType.REGULAR((3,)),
            dma((K,)), dma((K,)), dma((K,)), dma((K,)), dma((K,)), dma((K,)), dma((2, K)),
            dma((3,)), dma((3,)), dma((3,)), dma((3,)), dma((3,)), dma((3,)),
        ],
        compiler_params=pltpu.CompilerParams(collective_id=0, has_side_effects=True),
        name="window",
    )(rows_of(state), rows_of(costate), gates.reshape(768, 128))
    psi, lam, grads = pl.pallas_call(
        store_kernel,
        out_shape=tuple(jax.ShapeDtypeStruct(shape, F32) for shape in shapes),
        in_specs=[pl.BlockSpec(memory_space=pltpu.VMEM)] * 3,
        out_specs=[pl.BlockSpec(memory_space=pl.ANY)] * 3,
        scratch_shapes=[dma((3,))],
        name="store",
    )(*(pltpu.with_memory_space_constraint(r, pltpu.VMEM) for r in results))
    return field_of(psi), field_of(lam), grads.reshape(3, 2, 128, 128)


def solution(mesh):
    return jax.shard_map(
        on_device,
        mesh=mesh,
        in_specs=(P(None, "amp"), P(None, "amp"), P()),
        out_specs=(P(None, "amp"), P(None, "amp"), P()),
        check_vma=False,
    )
```

```python
import functools
import math

import jax
import jax.numpy as jnp
from jax import lax
from jax.experimental import pallas as pl
from jax.experimental.pallas import tpu as pltpu
from jax.sharding import PartitionSpec as P

F32 = jnp.float32
BF16 = jnp.bfloat16
MESH = pl.DeviceIdType.MESH
K = 4
PLANE = 32
NN = (((1,), (0,)), ((), ()))
NT = (((1,), (1,)), ((), ()))
TN = (((0,), (0,)), ((), ()))


def split(value):
    high = value.astype(BF16)
    return high, (value - high.astype(F32)).astype(BF16)


def dot3(stacked, high, low, dims):
    rows = stacked.shape[0] // 2
    both = lax.dot_general(stacked, high, dims, preferred_element_type=F32)
    rest = lax.dot_general(stacked[:rows], low, dims, preferred_element_type=F32)
    return both[:rows] + (both[rows:] + rest)


def kernel(
    scale, psi_hbm, lam_hbm, gates_hbm, psi_res, lam_res, gout,
    psi_in, lam_in, gates, mats, s1, r1, f1, s2, r2, f2, xb, zb, vh, vl, wh, wl, acc,
    terms, cb, hb, mr, yb,
    in_sem, entry_sem, st_send, st_recv, own_sem, red_send, red_recv,
):
    me = lax.axis_index("amp")
    y = me // PLANE
    m = lax.rem(me, PLANE)
    core = lax.rem(me, 2)
    x, z = m // 8, lax.rem(m // 2, 4)
    chip = m // 2
    barrier = pltpu.get_barrier_semaphore()

    def remote(src, dst, send, recv, device):
        return pltpu.make_async_remote_copy(
            src_ref=src, dst_ref=dst, send_sem=send, recv_sem=recv,
            device_id=(device,), device_id_type=MESH,
        )

    def peer(dx, dz, other):
        return lax.rem(x + dx, 4) * 8 + lax.rem(z + dz, 4) * 2 + lax.rem(core + other, 2)

    def at(dy, dx, dz, other):
        return lax.rem(y + dy, 4) * PLANE + peer(dx, dz, other)

    hops = (0, 1, 2, 1)
    offsets = [(dx, dz, o) for dx in range(4) for dz in range(4) for o in range(2)]
    offsets = sorted(offsets, key=lambda d: -(hops[d[0]] + hops[d[1]]))[:-2] + [(0, 0, 1)]
    same_core = [d for d in offsets if d[2] == 0]
    partner = at(0, 0, 0, 1)

    near = [(dy, 0, 0, 0) for dy in (2, 1, 3)]
    near += [(0, dx, 0, o) for dx in (1, 3) for o in range(2)]
    near += [(0, 0, dz, o) for dz in (1, 3) for o in range(2)] + [(0, 0, 0, 1)]
    rounds = (
        [(0, dx, 0, 0) for dx in (1, 3)],
        [(0, 0, dz, 0) for dz in (1, 3)],
        [(0, 0, dz, 0) for dz in (1, 3)],
    )

    def tell(semaphore, where):
        for offset in where:
            pl.semaphore_signal(
                semaphore, inc=1, device_id=(at(*offset),), device_id_type=MESH
            )

    def hear(i):
        pl.semaphore_wait(entry_sem.at[i], len(rounds[i]))

    loads = [
        pltpu.make_async_copy(gates_hbm.at[pl.ds(0, 256)], gates.at[pl.ds(0, 256)], in_sem.at[0]),
        pltpu.make_async_copy(psi_hbm, psi_in, in_sem.at[1]),
        pltpu.make_async_copy(lam_hbm, lam_in, in_sem.at[2]),
        pltpu.make_async_copy(
            gates_hbm.at[pl.ds(256, 512)], gates.at[pl.ds(256, 512)], in_sem.at[3]
        ),
    ]
    for load in loads:
        load.start()
    tell(barrier, near)

    def build(layer):
        real_t = gates[pl.ds(layer * 256, 128), :].T
        imag_t = gates[pl.ds(layer * 256 + 128, 128), :].T
        real_high, real_low = split(real_t)
        imag_high, imag_low = split(imag_t)
        for base, real, imag in ((0, real_high, imag_high), (256, real_low, imag_low)):
            mats[layer, base:base + 128, 0:128] = real
            mats[layer, base:base + 128, 128:256] = imag
            mats[layer, base + 128:base + 256, 0:128] = -imag
            mats[layer, base + 128:base + 256, 128:256] = real

    combos = [(a, b, p) for a in range(2) for b in range(2) for p in range(2)]
    ins = (psi_in, lam_in)
    outs = (psi_res, lam_res)

    def sub(array, block, part):
        return array * 4 + block * 2 + part

    def correlate(layer, first, lam, psi, dims):
        lam_high, lam_low = lam
        psi_high, psi_low = psi
        value = (
            lax.dot_general(lam_high, psi_high, dims, preferred_element_type=F32)
            + lax.dot_general(lam_high, psi_low, dims, preferred_element_type=F32)
            + lax.dot_general(lam_low, psi_high, dims, preferred_element_type=F32)
        )
        if first:
            acc[layer] = value
        else:
            acc[layer] += value

    def gate0(k, first):
        for a, b, p in combos:
            left = (a * 2 + b) * 128
            high, low = split(ins[a][pl.ds(k * 4 + b * 2 + p, 128, stride=16), :])
            vh[p * 128:p * 128 + 128, left:left + 128] = high
            vl[p * 128:p * 128 + 128, left:left + 128] = low
        value = dot3(mats[0], vh[...], vl[...], NN)
        for a, b, p in combos:
            left = (a * 2 + b) * 128
            part = value[p * 128:p * 128 + 128, left:left + 128]
            s1[k, pl.ds(sub(a, b, p), 128, stride=8), :] = part.T

    def grad0(k, first):
        correlate(
            0, first, (vh[:, 256:512], vl[:, 256:512]), (vh[:, 0:256], vl[:, 0:256]), NT
        )

    def load_rows(ref):
        for a, b, p in combos:
            top = (a * 2 + b) * 128
            high, low = split(ref[pl.ds(sub(a, b, p), 128, stride=8), :])
            wh[top:top + 128, p * 128:p * 128 + 128] = high
            wl[top:top + 128, p * 128:p * 128 + 128] = low

    def grad_rows(layer, first):
        correlate(layer, first, (wh[256:512], wl[256:512]), (wh[0:256], wl[0:256]), TN)

    f1_bits = f1.reshape(K, 2, 32, 2, 8, 128)
    xb_bits = xb.reshape(2, 32, 2, 8, 128)
    group = lax.broadcasted_iota(jnp.int32, (256, 128), 1) // 32

    def middle(k, first):
        parts = [f1_bits[k, i // 2, :, i % 2].reshape(256, 128) for i in range(4)]
        for j in range(4):
            turned = [
                parts[i] if i == j else pltpu.roll(parts[i], ((i - j) % 4) * 32, 1)
                for i in range(4)
            ]
            low_half = jnp.where(group == 0, turned[0], turned[1])
            high_half = jnp.where(group == 2, turned[2], turned[3])
            value = jnp.where(group < 2, low_half, high_half)
            xb_bits[j // 2, :, j % 2] = value.reshape(32, 8, 128)
        load_rows(xb)
        value = dot3(mats[1], wh[...], wl[...], NT)
        for a, b, p in combos:
            left = (a * 2 + b) * 128
            zb[pl.ds(sub(a, b, p), 128, stride=8), :] = (
                value[p * 128:p * 128 + 128, left:left + 128]
            )
        grad_rows(1, first)
        load_rows(zb)
        both = lax.dot_general(wh[...], mats[2], NT, preferred_element_type=F32)
        rest = lax.dot_general(wl[...], mats[2, 0:256], NT, preferred_element_type=F32)
        value = both[:, 0:256] + (both[:, 256:512] + rest)
        for a, b, p in combos:
            top = (a * 2 + b) * 128
            s2[k, pl.ds(sub(a, b, p), 128, stride=8), :] = (
                value[top:top + 128, p * 128:p * 128 + 128]
            )

    def finish(k):
        for a, b, p in combos:
            outs[a][pl.ds(k * 4 + b * 2 + p, 128, stride=16), :] = (
                f2[k, pl.ds(sub(a, b, p), 128, stride=8), :].T
            )

    def tiles(ref):
        return ref.reshape(K, 4, PLANE, 8, 128)

    def plane_start(st, src, dst, k):
        src_t, dst_t = tiles(src), tiles(dst)
        for offset in offsets:
            q = peer(*offset)
            remote(
                src_t.at[k, :, q], dst_t.at[k, :, m],
                st_send.at[st, k], st_recv.at[st, k], y * PLANE + q,
            ).start()
        pltpu.make_async_copy(src_t.at[k, :, m], dst_t.at[k, :, m], own_sem.at[st, k]).start()

    def plane_wait(st, src, dst, k, arrived=True):
        whole = remote(
            src.at[k, pl.ds(0, 992)], dst.at[k, pl.ds(0, 992)],
            st_send.at[st, k], st_recv.at[st, k], partner,
        )
        if not arrived:
            whole.wait_send()
            return
        whole.wait_recv()
        src_t, dst_t = tiles(src), tiles(dst)
        pltpu.make_async_copy(src_t.at[k, :, m], dst_t.at[k, :, m], own_sem.at[st, k]).wait()

    def y_start(st, src, dst, k):
        src_t, dst_t = tiles(src), tiles(dst)
        for step in (2, 1, 3):
            to = lax.rem(y + step, 4)
            remote(
                src_t.at[k, to], dst_t.at[k, y],
                st_send.at[st, k], st_recv.at[st, k], to * PLANE + m,
            ).start()
        pltpu.make_async_copy(src_t.at[k, y], dst_t.at[k, y], own_sem.at[st, k]).start()

    def y_wait(st, src, dst, k, arrived=True):
        whole = remote(
            src.at[k, pl.ds(0, 768)], dst.at[k, pl.ds(0, 768)],
            st_send.at[st, k], st_recv.at[st, k], partner,
        )
        if not arrived:
            whole.wait_send()
            return
        whole.wait_recv()
        src_t, dst_t = tiles(src), tiles(dst)
        pltpu.make_async_copy(src_t.at[k, y], dst_t.at[k, y], own_sem.at[st, k]).wait()

    buffers = ((s1, r1), (r1, f1), (s2, r2), (r2, f2))
    y_stage = [[k % 2 == (0 if st in (0, 3) else 1) for k in range(K)] for st in range(4)]

    def go(st, k):
        (y_start if y_stage[st][k] else plane_start)(st, *buffers[st], k)

    def got(st, k, arrived=True):
        (y_wait if y_stage[st][k] else plane_wait)(st, *buffers[st], k, arrived)

    def red(step, layer, src, dst, device):
        return remote(
            src, dst, red_send.at[step, layer], red_recv.at[step, layer], device
        )

    mine = pl.ds((core * 16 + chip) * 8, 8)
    slot = pl.ds(chip * 8, 8)
    y_slot = pl.ds(y * 8, 8)
    own_half = pl.ds(core * 128, 128)
    other_half = pl.ds((1 - core) * 128, 128)

    def pair_copy(layer):
        return red(0, layer, terms.at[layer, other_half], cb.at[layer], partner)

    def back_copy(layer):
        return red(4, layer, gout.at[layer, own_half], gout.at[layer, own_half], partner)

    def all_of(step, layer):
        if step == 0:
            return pair_copy(layer)
        if step == 1:
            part = pl.ds(0, 120)
            return red(1, layer, hb.at[layer, part], mr.at[layer, part], partner)
        if step == 2:
            part = pl.ds(0, 24)
            return red(2, layer, yb.at[layer, part], yb.at[layer, part], partner)
        if step == 3:
            part = pl.ds(0, 120)
            return red(3, layer, gout.at[layer, part], gout.at[layer, part], partner)
        return back_copy(layer)

    def reduce0(layer):
        real = acc[layer, 0:128, 0:128] + acc[layer, 128:256, 128:256]
        imag = acc[layer, 128:256, 0:128] - acc[layer, 0:128, 128:256]
        high, low = split(jnp.concatenate([real, -imag], axis=1))
        left = lax.dot_general(high, mats[layer], NT, preferred_element_type=F32)
        rest = lax.dot_general(low, mats[layer, 0:256], NT, preferred_element_type=F32)
        value = left[:, 0:256] + (left[:, 256:512] + rest)
        terms[layer, 0:128, :] = value[:, 0:128]
        terms[layer, 128:256, :] = -value[:, 128:256]
        pair_copy(layer).start()

    def reduce1(layer):
        all_of(0, layer).wait_recv()
        hb[layer] = terms[layer, own_half, :] + cb[layer]
        mr[layer, slot, :] = hb[layer, slot, :]
        for offset in same_core:
            q = peer(*offset)
            red(
                1, layer, hb.at[layer, pl.ds((q // 2) * 8, 8)], mr.at[layer, slot],
                y * PLANE + q,
            ).start()

    def reduce2(layer):
        all_of(1, layer).wait_recv()
        parts = [mr[layer, i * 8:i * 8 + 8, :] for i in range(16)]
        while len(parts) > 1:
            parts = [parts[i] + parts[i + 1] for i in range(0, len(parts), 2)]
        yb[layer, y_slot, :] = parts[0]
        for step in (2, 1, 3):
            red(
                2, layer, yb.at[layer, y_slot], yb.at[layer, y_slot],
                lax.rem(y + step, 4) * PLANE + m,
            ).start()

    def reduce3(layer):
        all_of(2, layer).wait_recv()
        total = (yb[layer, 0:8, :] + yb[layer, 8:16, :]) + (
            yb[layer, 16:24, :] + yb[layer, 24:32, :]
        )
        gout[layer, mine, :] = total * scale
        for offset in same_core:
            red(
                3, layer, gout.at[layer, mine], gout.at[layer, mine],
                y * PLANE + peer(*offset),
            ).start()

    def reduce4(layer):
        all_of(3, layer).wait_recv()
        back_copy(layer).start()

    def reduce5(layer):
        all_of(4, layer).wait_recv()

    loads[0].wait()
    build(0)
    loads[1].wait()
    loads[2].wait()
    gate0(0, True)
    pl.semaphore_wait(barrier, len(near))
    tell(entry_sem.at[0], rounds[0])
    go(0, 0)
    grad0(0, True)
    gate0(1, False)
    hear(0)
    tell(entry_sem.at[1], rounds[1])
    grad0(1, False)
    hear(1)
    tell(entry_sem.at[2], rounds[2])
    hear(2)
    go(0, 1)
    gate0(2, False)
    go(0, 2)
    grad0(2, False)
    gate0(3, False)
    go(0, 3)
    grad0(3, False)
    loads[3].wait()
    build(1)
    build(2)
    reduce0(0)
    got(0, 0)
    go(1, 0)
    reduce1(0)
    got(0, 1)
    go(1, 1)
    got(0, 2)
    go(1, 2)
    got(0, 3)
    go(1, 3)
    got(1, 1)
    middle(1, True)
    go(2, 1)
    grad_rows(2, True)
    got(1, 0)
    middle(0, False)
    go(2, 0)
    grad_rows(2, False)
    reduce2(0)
    got(1, 3)
    middle(3, False)
    go(2, 3)
    grad_rows(2, False)
    got(1, 2)
    middle(2, False)
    grad_rows(2, False)
    reduce0(2)
    reduce0(1)
    reduce1(2)
    reduce1(1)
    go(2, 2)
    got(2, 1)
    go(3, 1)
    reduce3(0)
    got(2, 0)
    reduce2(2)
    reduce2(1)
    go(3, 0)
    got(2, 3)
    reduce3(2)
    reduce3(1)
    go(3, 3)
    got(2, 2)
    go(3, 2)
    reduce4(0)
    got(3, 1)
    finish(1)
    got(3, 0)
    finish(0)
    reduce4(2)
    reduce4(1)
    got(3, 2)
    finish(2)
    got(3, 3)
    finish(3)
    for layer in range(3):
        reduce5(layer)

    for st in range(4):
        for k in range(K):
            got(st, k, False)
    for step in range(5):
        for layer in range(3):
            all_of(step, layer).wait_send()


def store_kernel(psi_res, lam_res, gout, psi_out, lam_out, grad_out, sem):
    copies = [
        pltpu.make_async_copy(src, dst, sem.at[i])
        for i, (src, dst) in enumerate(((psi_res, psi_out), (lam_res, lam_out), (gout, grad_out)))
    ]
    for copy in copies:
        copy.start()
    for copy in copies:
        copy.wait()


def rows_of(field):
    return field.reshape(2, 1024, 128).transpose(1, 0, 2).reshape(2048, 128)


def field_of(rows):
    return rows.reshape(1024, 2, 128).transpose(1, 0, 2).reshape(2, 131072)


def on_device(state, costate, gates):
    scale = 1.0 / math.sqrt(128 * 1024)
    dma = pltpu.SemaphoreType.DMA
    shapes = ((2048, 128), (2048, 128), (3, 256, 128))
    results = pl.pallas_call(
        functools.partial(kernel, scale),
        out_shape=tuple(pltpu.VMEM(shape, F32) for shape in shapes),
        in_specs=[pl.BlockSpec(memory_space=pl.ANY)] * 3,
        out_specs=[pl.BlockSpec(memory_space=pltpu.VMEM)] * 3,
        scratch_shapes=[
            pltpu.VMEM((2048, 128), F32),
            pltpu.VMEM((2048, 128), F32),
            pltpu.VMEM((768, 128), F32),
            pltpu.VMEM((3, 512, 256), BF16),
        ]
        + [pltpu.VMEM((K, 1024, 128), F32)] * 6
        + [
            pltpu.VMEM((1024, 128), F32),
            pltpu.VMEM((1024, 128), F32),
            pltpu.VMEM((256, 512), BF16),
            pltpu.VMEM((256, 512), BF16),
            pltpu.VMEM((512, 256), BF16),
            pltpu.VMEM((512, 256), BF16),
            pltpu.VMEM((3, 256, 256), F32),
            pltpu.VMEM((3, 256, 128), F32),
            pltpu.VMEM((3, 128, 128), F32),
            pltpu.VMEM((3, 128, 128), F32),
            pltpu.VMEM((3, 128, 128), F32),
            pltpu.VMEM((3, 32, 128), F32),
            dma((4,)), pltpu.SemaphoreType.REGULAR((3,)),
            dma((4, K)), dma((4, K)), dma((4, K)), dma((5, 3)), dma((5, 3)),
        ],
        compiler_params=pltpu.CompilerParams(collective_id=0, has_side_effects=True),
        name="window",
    )(rows_of(state), rows_of(costate), gates.reshape(768, 128))
    psi, lam, grads = pl.pallas_call(
        store_kernel,
        out_shape=tuple(jax.ShapeDtypeStruct(shape, F32) for shape in shapes),
        in_specs=[pl.BlockSpec(memory_space=pltpu.VMEM)] * 3,
        out_specs=[pl.BlockSpec(memory_space=pl.ANY)] * 3,
        scratch_shapes=[dma((3,))],
        name="store",
    )(*(pltpu.with_memory_space_constraint(r, pltpu.VMEM) for r in results))
    return field_of(psi), field_of(lam), grads.reshape(3, 2, 128, 128)


def solution(mesh):
    return jax.shard_map(
        on_device,
        mesh=mesh,
        in_specs=(P(None, "amp"), P(None, "amp"), P()),
        out_specs=(P(None, "amp"), P(None, "amp"), P()),
        check_vma=False,
    )
```

```python
import functools
import math

import jax
import jax.numpy as jnp
from jax import lax
from jax.experimental import pallas as pl
from jax.experimental.pallas import tpu as pltpu
from jax.sharding import PartitionSpec as P

F32 = jnp.float32
BF16 = jnp.bfloat16
MESH = pl.DeviceIdType.MESH
K = 4
PLANE = 32
NN = (((1,), (0,)), ((), ()))
NT = (((1,), (1,)), ((), ()))
TN = (((0,), (0,)), ((), ()))


def split(value):
    high = value.astype(BF16)
    return high, (value - high.astype(F32)).astype(BF16)


def dot3(stacked, high, low, dims):
    rows = stacked.shape[0] // 2
    both = lax.dot_general(stacked, high, dims, preferred_element_type=F32)
    rest = lax.dot_general(stacked[:rows], low, dims, preferred_element_type=F32)
    return both[:rows] + (both[rows:] + rest)


def kernel(
    scale, psi_hbm, lam_hbm, gates_hbm, psi_res, lam_res, gout,
    psi_in, lam_in, gates, mats, s1, r1, f1, s2, r2, f2, xb, zb, vh, vl, wh, wl, acc,
    terms, cb, hb, mr, yb,
    in_sem, entry_sem, st_send, st_recv, own_sem, red_send, red_recv,
):
    me = lax.axis_index("amp")
    y = me // PLANE
    m = lax.rem(me, PLANE)
    core = lax.rem(me, 2)
    x, z = m // 8, lax.rem(m // 2, 4)
    chip = m // 2
    barrier = pltpu.get_barrier_semaphore()

    def remote(src, dst, send, recv, device):
        return pltpu.make_async_remote_copy(
            src_ref=src, dst_ref=dst, send_sem=send, recv_sem=recv,
            device_id=(device,), device_id_type=MESH,
        )

    def peer(dx, dz, other):
        return lax.rem(x + dx, 4) * 8 + lax.rem(z + dz, 4) * 2 + lax.rem(core + other, 2)

    def at(dy, dx, dz, other):
        return lax.rem(y + dy, 4) * PLANE + peer(dx, dz, other)

    hops = (0, 1, 2, 1)
    offsets = [(dx, dz, o) for dx in range(4) for dz in range(4) for o in range(2)]
    offsets = sorted(offsets, key=lambda d: -(hops[d[0]] + hops[d[1]]))[:-2] + [(0, 0, 1)]
    same_core = [d for d in offsets if d[2] == 0]
    partner = at(0, 0, 0, 1)

    near = [(dy, 0, 0, 0) for dy in (2, 1, 3)]
    near += [(0, dx, 0, o) for dx in (1, 3) for o in range(2)]
    near += [(0, 0, dz, o) for dz in (1, 3) for o in range(2)] + [(0, 0, 0, 1)]
    rounds = (
        [(0, dx, 0, 0) for dx in (1, 3)] + [(0, 0, dz, 0) for dz in (1, 3)],
        [(0, 2, 0, 0), (0, 0, 2, 0)],
    )

    def reach(d):
        return hops[d[0]] + hops[d[1]]

    known = [[d for d in offsets if reach(d) in span] for span in ((0, 1), (2,), (3, 4))]

    def tell(semaphore, where):
        for offset in where:
            pl.semaphore_signal(
                semaphore, inc=1, device_id=(at(*offset),), device_id_type=MESH
            )

    def hear(i):
        pl.semaphore_wait(entry_sem.at[i], len(rounds[i]))

    loads = [
        pltpu.make_async_copy(gates_hbm.at[pl.ds(0, 256)], gates.at[pl.ds(0, 256)], in_sem.at[0]),
        pltpu.make_async_copy(psi_hbm, psi_in, in_sem.at[1]),
        pltpu.make_async_copy(lam_hbm, lam_in, in_sem.at[2]),
        pltpu.make_async_copy(
            gates_hbm.at[pl.ds(256, 512)], gates.at[pl.ds(256, 512)], in_sem.at[3]
        ),
    ]
    for load in loads:
        load.start()
    tell(barrier, near)

    def build(layer):
        real_t = gates[pl.ds(layer * 256, 128), :].T
        imag_t = gates[pl.ds(layer * 256 + 128, 128), :].T
        real_high, real_low = split(real_t)
        imag_high, imag_low = split(imag_t)
        for base, real, imag in ((0, real_high, imag_high), (256, real_low, imag_low)):
            mats[layer, base:base + 128, 0:128] = real
            mats[layer, base:base + 128, 128:256] = imag
            mats[layer, base + 128:base + 256, 0:128] = -imag
            mats[layer, base + 128:base + 256, 128:256] = real

    combos = [(a, b, p) for a in range(2) for b in range(2) for p in range(2)]
    ins = (psi_in, lam_in)
    outs = (psi_res, lam_res)

    def sub(array, block, part):
        return array * 4 + block * 2 + part

    def correlate(layer, first, lam, psi, dims):
        lam_high, lam_low = lam
        psi_high, psi_low = psi
        value = (
            lax.dot_general(lam_high, psi_high, dims, preferred_element_type=F32)
            + lax.dot_general(lam_high, psi_low, dims, preferred_element_type=F32)
            + lax.dot_general(lam_low, psi_high, dims, preferred_element_type=F32)
        )
        if first:
            acc[layer] = value
        else:
            acc[layer] += value

    def gate0(k, first):
        for a, b, p in combos:
            left = (a * 2 + b) * 128
            high, low = split(ins[a][pl.ds(k * 4 + b * 2 + p, 128, stride=16), :])
            vh[p * 128:p * 128 + 128, left:left + 128] = high
            vl[p * 128:p * 128 + 128, left:left + 128] = low
        value = dot3(mats[0], vh[...], vl[...], NN)
        for a, b, p in combos:
            left = (a * 2 + b) * 128
            part = value[p * 128:p * 128 + 128, left:left + 128]
            s1[k, pl.ds(sub(a, b, p), 128, stride=8), :] = part.T

    def grad0(k, first):
        correlate(
            0, first, (vh[:, 256:512], vl[:, 256:512]), (vh[:, 0:256], vl[:, 0:256]), NT
        )

    def load_rows(ref):
        for a, b, p in combos:
            top = (a * 2 + b) * 128
            high, low = split(ref[pl.ds(sub(a, b, p), 128, stride=8), :])
            wh[top:top + 128, p * 128:p * 128 + 128] = high
            wl[top:top + 128, p * 128:p * 128 + 128] = low

    def grad_rows(layer, first):
        correlate(layer, first, (wh[256:512], wl[256:512]), (wh[0:256], wl[0:256]), TN)

    f1_bits = f1.reshape(K, 2, 32, 2, 8, 128)
    xb_bits = xb.reshape(2, 32, 2, 8, 128)
    group = lax.broadcasted_iota(jnp.int32, (256, 128), 1) // 32

    def middle(k, first):
        parts = [f1_bits[k, i // 2, :, i % 2].reshape(256, 128) for i in range(4)]
        for j in range(4):
            turned = [
                parts[i] if i == j else pltpu.roll(parts[i], ((i - j) % 4) * 32, 1)
                for i in range(4)
            ]
            low_half = jnp.where(group == 0, turned[0], turned[1])
            high_half = jnp.where(group == 2, turned[2], turned[3])
            value = jnp.where(group < 2, low_half, high_half)
            xb_bits[j // 2, :, j % 2] = value.reshape(32, 8, 128)
        load_rows(xb)
        value = dot3(mats[1], wh[...], wl[...], NT)
        for a, b, p in combos:
            left = (a * 2 + b) * 128
            zb[pl.ds(sub(a, b, p), 128, stride=8), :] = (
                value[p * 128:p * 128 + 128, left:left + 128]
            )
        grad_rows(1, first)
        load_rows(zb)
        both = lax.dot_general(wh[...], mats[2], NT, preferred_element_type=F32)
        rest = lax.dot_general(wl[...], mats[2, 0:256], NT, preferred_element_type=F32)
        value = both[:, 0:256] + (both[:, 256:512] + rest)
        for a, b, p in combos:
            top = (a * 2 + b) * 128
            s2[k, pl.ds(sub(a, b, p), 128, stride=8), :] = (
                value[top:top + 128, p * 128:p * 128 + 128]
            )

    def finish(k):
        for a, b, p in combos:
            outs[a][pl.ds(k * 4 + b * 2 + p, 128, stride=16), :] = (
                f2[k, pl.ds(sub(a, b, p), 128, stride=8), :].T
            )

    def tiles(ref):
        return ref.reshape(K, 4, PLANE, 8, 128)

    def plane_start(st, src, dst, k, where=offsets):
        src_t, dst_t = tiles(src), tiles(dst)
        for offset in where:
            q = peer(*offset)
            remote(
                src_t.at[k, :, q], dst_t.at[k, :, m],
                st_send.at[st, k], st_recv.at[st, k], y * PLANE + q,
            ).start()
        if where[-1] == (0, 0, 1):
            own = pltpu.make_async_copy(src_t.at[k, :, m], dst_t.at[k, :, m], own_sem.at[st, k])
            own.start()

    def plane_wait(st, src, dst, k, arrived=True):
        whole = remote(
            src.at[k, pl.ds(0, 992)], dst.at[k, pl.ds(0, 992)],
            st_send.at[st, k], st_recv.at[st, k], partner,
        )
        if not arrived:
            whole.wait_send()
            return
        whole.wait_recv()
        src_t, dst_t = tiles(src), tiles(dst)
        pltpu.make_async_copy(src_t.at[k, :, m], dst_t.at[k, :, m], own_sem.at[st, k]).wait()

    def y_start(st, src, dst, k):
        src_t, dst_t = tiles(src), tiles(dst)
        for step in (2, 1, 3):
            to = lax.rem(y + step, 4)
            remote(
                src_t.at[k, to], dst_t.at[k, y],
                st_send.at[st, k], st_recv.at[st, k], to * PLANE + m,
            ).start()
        pltpu.make_async_copy(src_t.at[k, y], dst_t.at[k, y], own_sem.at[st, k]).start()

    def y_wait(st, src, dst, k, arrived=True):
        whole = remote(
            src.at[k, pl.ds(0, 768)], dst.at[k, pl.ds(0, 768)],
            st_send.at[st, k], st_recv.at[st, k], partner,
        )
        if not arrived:
            whole.wait_send()
            return
        whole.wait_recv()
        src_t, dst_t = tiles(src), tiles(dst)
        pltpu.make_async_copy(src_t.at[k, y], dst_t.at[k, y], own_sem.at[st, k]).wait()

    buffers = ((s1, r1), (r1, f1), (s2, r2), (r2, f2))
    y_stage = [[k % 2 == (0 if st in (0, 3) else 1) for k in range(K)] for st in range(4)]

    def go(st, k):
        (y_start if y_stage[st][k] else plane_start)(st, *buffers[st], k)

    def got(st, k, arrived=True):
        (y_wait if y_stage[st][k] else plane_wait)(st, *buffers[st], k, arrived)

    def red(step, layer, src, dst, device):
        return remote(
            src, dst, red_send.at[step, layer], red_recv.at[step, layer], device
        )

    mine = pl.ds((core * 16 + chip) * 8, 8)
    slot = pl.ds(chip * 8, 8)
    y_slot = pl.ds(y * 8, 8)
    own_half = pl.ds(core * 128, 128)
    other_half = pl.ds((1 - core) * 128, 128)

    def pair_copy(layer):
        return red(0, layer, terms.at[layer, other_half], cb.at[layer], partner)

    def back_copy(layer):
        return red(4, layer, gout.at[layer, own_half], gout.at[layer, own_half], partner)

    def all_of(step, layer):
        if step == 0:
            return pair_copy(layer)
        if step == 1:
            part = pl.ds(0, 120)
            return red(1, layer, hb.at[layer, part], mr.at[layer, part], partner)
        if step == 2:
            part = pl.ds(0, 24)
            return red(2, layer, yb.at[layer, part], yb.at[layer, part], partner)
        if step == 3:
            part = pl.ds(0, 120)
            return red(3, layer, gout.at[layer, part], gout.at[layer, part], partner)
        return back_copy(layer)

    def reduce0(layer):
        real = acc[layer, 0:128, 0:128] + acc[layer, 128:256, 128:256]
        imag = acc[layer, 128:256, 0:128] - acc[layer, 0:128, 128:256]
        high, low = split(jnp.concatenate([real, -imag], axis=1))
        left = lax.dot_general(high, mats[layer], NT, preferred_element_type=F32)
        rest = lax.dot_general(low, mats[layer, 0:256], NT, preferred_element_type=F32)
        value = left[:, 0:256] + (left[:, 256:512] + rest)
        terms[layer, 0:128, :] = value[:, 0:128]
        terms[layer, 128:256, :] = -value[:, 128:256]
        pair_copy(layer).start()

    def reduce1(layer):
        all_of(0, layer).wait_recv()
        hb[layer] = terms[layer, own_half, :] + cb[layer]
        mr[layer, slot, :] = hb[layer, slot, :]
        for offset in same_core:
            q = peer(*offset)
            red(
                1, layer, hb.at[layer, pl.ds((q // 2) * 8, 8)], mr.at[layer, slot],
                y * PLANE + q,
            ).start()

    def reduce2(layer):
        all_of(1, layer).wait_recv()
        parts = [mr[layer, i * 8:i * 8 + 8, :] for i in range(16)]
        while len(parts) > 1:
            parts = [parts[i] + parts[i + 1] for i in range(0, len(parts), 2)]
        yb[layer, y_slot, :] = parts[0]
        for step in (2, 1, 3):
            red(
                2, layer, yb.at[layer, y_slot], yb.at[layer, y_slot],
                lax.rem(y + step, 4) * PLANE + m,
            ).start()

    def reduce3(layer):
        all_of(2, layer).wait_recv()
        total = (yb[layer, 0:8, :] + yb[layer, 8:16, :]) + (
            yb[layer, 16:24, :] + yb[layer, 24:32, :]
        )
        gout[layer, mine, :] = total * scale
        for offset in same_core:
            red(
                3, layer, gout.at[layer, mine], gout.at[layer, mine],
                y * PLANE + peer(*offset),
            ).start()

    def reduce4(layer):
        all_of(3, layer).wait_recv()
        back_copy(layer).start()

    def reduce5(layer):
        all_of(4, layer).wait_recv()

    loads[0].wait()
    build(0)
    loads[1].wait()
    loads[2].wait()
    gate0(1, True)
    pl.semaphore_wait(barrier, len(near))
    tell(entry_sem.at[0], rounds[0])
    plane_start(0, s1, r1, 1, known[0])
    grad0(1, True)
    gate0(0, False)
    go(0, 0)
    hear(0)
    tell(entry_sem.at[1], rounds[1])
    plane_start(0, s1, r1, 1, known[1])
    grad0(0, False)
    gate0(2, False)
    go(0, 2)
    hear(1)
    plane_start(0, s1, r1, 1, known[2])
    grad0(2, False)
    gate0(3, False)
    go(0, 3)
    grad0(3, False)
    loads[3].wait()
    build(1)
    build(2)
    reduce0(0)
    got(0, 0)
    go(1, 0)
    reduce1(0)
    got(0, 1)
    go(1, 1)
    got(0, 2)
    go(1, 2)
    got(0, 3)
    go(1, 3)
    got(1, 1)
    middle(1, True)
    go(2, 1)
    grad_rows(2, True)
    got(1, 0)
    middle(0, False)
    go(2, 0)
    grad_rows(2, False)
    reduce2(0)
    got(1, 3)
    middle(3, False)
    go(2, 3)
    grad_rows(2, False)
    got(1, 2)
    middle(2, False)
    go(2, 2)
    grad_rows(2, False)
    reduce0(2)
    reduce0(1)
    reduce1(2)
    reduce1(1)
    got(2, 1)
    go(3, 1)
    reduce3(0)
    got(2, 0)
    go(3, 0)
    reduce2(2)
    reduce2(1)
    got(2, 3)
    go(3, 3)
    got(2, 2)
    go(3, 2)
    reduce3(2)
    reduce3(1)
    reduce4(0)
    got(3, 1)
    finish(1)
    got(3, 0)
    finish(0)
    reduce4(2)
    reduce4(1)
    got(3, 2)
    finish(2)
    got(3, 3)
    finish(3)
    for layer in range(3):
        reduce5(layer)

    for st in range(4):
        for k in range(K):
            got(st, k, False)
    for step in range(5):
        for layer in range(3):
            all_of(step, layer).wait_send()


def store_kernel(psi_res, lam_res, gout, psi_out, lam_out, grad_out, sem):
    copies = [
        pltpu.make_async_copy(src, dst, sem.at[i])
        for i, (src, dst) in enumerate(((psi_res, psi_out), (lam_res, lam_out), (gout, grad_out)))
    ]
    for copy in copies:
        copy.start()
    for copy in copies:
        copy.wait()


def rows_of(field):
    return field.reshape(2, 1024, 128).transpose(1, 0, 2).reshape(2048, 128)


def field_of(rows):
    return rows.reshape(1024, 2, 128).transpose(1, 0, 2).reshape(2, 131072)


def on_device(state, costate, gates):
    scale = 1.0 / math.sqrt(128 * 1024)
    dma = pltpu.SemaphoreType.DMA
    shapes = ((2048, 128), (2048, 128), (3, 256, 128))
    results = pl.pallas_call(
        functools.partial(kernel, scale),
        out_shape=tuple(pltpu.VMEM(shape, F32) for shape in shapes),
        in_specs=[pl.BlockSpec(memory_space=pl.ANY)] * 3,
        out_specs=[pl.BlockSpec(memory_space=pltpu.VMEM)] * 3,
        scratch_shapes=[
            pltpu.VMEM((2048, 128), F32),
            pltpu.VMEM((2048, 128), F32),
            pltpu.VMEM((768, 128), F32),
            pltpu.VMEM((3, 512, 256), BF16),
        ]
        + [pltpu.VMEM((K, 1024, 128), F32)] * 6
        + [
            pltpu.VMEM((1024, 128), F32),
            pltpu.VMEM((1024, 128), F32),
            pltpu.VMEM((256, 512), BF16),
            pltpu.VMEM((256, 512), BF16),
            pltpu.VMEM((512, 256), BF16),
            pltpu.VMEM((512, 256), BF16),
            pltpu.VMEM((3, 256, 256), F32),
            pltpu.VMEM((3, 256, 128), F32),
            pltpu.VMEM((3, 128, 128), F32),
            pltpu.VMEM((3, 128, 128), F32),
            pltpu.VMEM((3, 128, 128), F32),
            pltpu.VMEM((3, 32, 128), F32),
            dma((4,)), pltpu.SemaphoreType.REGULAR((2,)),
            dma((4, K)), dma((4, K)), dma((4, K)), dma((5, 3)), dma((5, 3)),
        ],
        compiler_params=pltpu.CompilerParams(collective_id=0, has_side_effects=True),
        name="window",
    )(rows_of(state), rows_of(costate), gates.reshape(768, 128))
    psi, lam, grads = pl.pallas_call(
        store_kernel,
        out_shape=tuple(jax.ShapeDtypeStruct(shape, F32) for shape in shapes),
        in_specs=[pl.BlockSpec(memory_space=pltpu.VMEM)] * 3,
        out_specs=[pl.BlockSpec(memory_space=pl.ANY)] * 3,
        scratch_shapes=[dma((3,))],
        name="store",
    )(*(pltpu.with_memory_space_constraint(r, pltpu.VMEM) for r in results))
    return field_of(psi), field_of(lam), grads.reshape(3, 2, 128, 128)


def solution(mesh):
    return jax.shard_map(
        on_device,
        mesh=mesh,
        in_specs=(P(None, "amp"), P(None, "amp"), P()),
        out_specs=(P(None, "amp"), P(None, "amp"), P()),
        check_vma=False,
    )
```

```python
import functools
import math

import jax
import jax.numpy as jnp
from jax import lax
from jax.experimental import pallas as pl
from jax.experimental.pallas import tpu as pltpu
from jax.sharding import PartitionSpec as P

F32 = jnp.float32
BF16 = jnp.bfloat16
MESH = pl.DeviceIdType.MESH
K = 4
PLANE = 32
NN = (((1,), (0,)), ((), ()))
NT = (((1,), (1,)), ((), ()))
TN = (((0,), (0,)), ((), ()))


def split(value):
    high = value.astype(BF16)
    return high, (value - high.astype(F32)).astype(BF16)


def dot3(stacked, high, low, dims):
    rows = stacked.shape[0] // 2
    both = lax.dot_general(stacked, high, dims, preferred_element_type=F32)
    rest = lax.dot_general(stacked[:rows], low, dims, preferred_element_type=F32)
    return both[:rows] + (both[rows:] + rest)


def kernel(
    scale, psi_hbm, lam_hbm, gates_hbm, psi_res, lam_res, gout,
    psi_in, lam_in, gates, mats, s1, r1, f1, s2, r2, f2, xb, zb, vh, vl, wh, wl, acc,
    terms, cb, hb, mr, yb,
    in_sem, entry_sem, st_send, st_recv, own_sem, red_send, red_recv,
):
    me = lax.axis_index("amp")
    y = me // PLANE
    m = lax.rem(me, PLANE)
    core = lax.rem(me, 2)
    x, z = m // 8, lax.rem(m // 2, 4)
    chip = m // 2
    barrier = pltpu.get_barrier_semaphore()

    def remote(src, dst, send, recv, device):
        return pltpu.make_async_remote_copy(
            src_ref=src, dst_ref=dst, send_sem=send, recv_sem=recv,
            device_id=(device,), device_id_type=MESH,
        )

    def peer(dx, dz, other):
        return lax.rem(x + dx, 4) * 8 + lax.rem(z + dz, 4) * 2 + lax.rem(core + other, 2)

    def at(dy, dx, dz, other):
        return lax.rem(y + dy, 4) * PLANE + peer(dx, dz, other)

    hops = (0, 1, 2, 1)
    offsets = [(dx, dz, o) for dx in range(4) for dz in range(4) for o in range(2)]
    offsets = sorted(offsets, key=lambda d: -(hops[d[0]] + hops[d[1]]))[:-2] + [(0, 0, 1)]
    same_core = [d for d in offsets if d[2] == 0]
    bulk = sorted(offsets[:-1], key=lambda d: ((d[0] + d[1]) % 4, d[2], d[0])) + offsets[-1:]
    partner = at(0, 0, 0, 1)

    near = [(dy, 0, 0, 0) for dy in (2, 1, 3)]
    near += [(0, dx, 0, o) for dx in (1, 3) for o in range(2)]
    near += [(0, 0, dz, o) for dz in (1, 3) for o in range(2)] + [(0, 0, 0, 1)]
    rounds = (
        [(0, dx, 0, 0) for dx in (1, 3)] + [(0, 0, dz, 0) for dz in (1, 3)],
        [(0, 2, 0, 0), (0, 0, 2, 0)],
    )

    def reach(d):
        return hops[d[0]] + hops[d[1]]

    known = [[d for d in offsets if reach(d) in span] for span in ((0, 1), (2,), (3, 4))]

    def tell(semaphore, where):
        for offset in where:
            pl.semaphore_signal(
                semaphore, inc=1, device_id=(at(*offset),), device_id_type=MESH
            )

    def hear(i):
        pl.semaphore_wait(entry_sem.at[i], len(rounds[i]))

    loads = [
        pltpu.make_async_copy(gates_hbm.at[pl.ds(0, 256)], gates.at[pl.ds(0, 256)], in_sem.at[0]),
        pltpu.make_async_copy(psi_hbm, psi_in, in_sem.at[1]),
        pltpu.make_async_copy(lam_hbm, lam_in, in_sem.at[2]),
        pltpu.make_async_copy(
            gates_hbm.at[pl.ds(256, 512)], gates.at[pl.ds(256, 512)], in_sem.at[3]
        ),
    ]
    for load in loads:
        load.start()
    tell(barrier, near)

    def build(layer):
        real_t = gates[pl.ds(layer * 256, 128), :].T
        imag_t = gates[pl.ds(layer * 256 + 128, 128), :].T
        real_high, real_low = split(real_t)
        imag_high, imag_low = split(imag_t)
        for base, real, imag in ((0, real_high, imag_high), (256, real_low, imag_low)):
            mats[layer, base:base + 128, 0:128] = real
            mats[layer, base:base + 128, 128:256] = imag
            mats[layer, base + 128:base + 256, 0:128] = -imag
            mats[layer, base + 128:base + 256, 128:256] = real

    combos = [(a, b, p) for a in range(2) for b in range(2) for p in range(2)]
    ins = (psi_in, lam_in)
    outs = (psi_res, lam_res)

    def sub(array, block, part):
        return array * 4 + block * 2 + part

    def correlate(layer, first, lam, psi, dims):
        lam_high, lam_low = lam
        psi_high, psi_low = psi
        value = (
            lax.dot_general(lam_high, psi_high, dims, preferred_element_type=F32)
            + lax.dot_general(lam_high, psi_low, dims, preferred_element_type=F32)
            + lax.dot_general(lam_low, psi_high, dims, preferred_element_type=F32)
        )
        if first:
            acc[layer] = value
        else:
            acc[layer] += value

    def gate0(k, first):
        for a, b, p in combos:
            left = (a * 2 + b) * 128
            high, low = split(ins[a][pl.ds(k * 4 + b * 2 + p, 128, stride=16), :])
            vh[p * 128:p * 128 + 128, left:left + 128] = high
            vl[p * 128:p * 128 + 128, left:left + 128] = low
        value = dot3(mats[0], vh[...], vl[...], NN)
        for a, b, p in combos:
            left = (a * 2 + b) * 128
            part = value[p * 128:p * 128 + 128, left:left + 128]
            s1[k, pl.ds(sub(a, b, p), 128, stride=8), :] = part.T

    def grad0(k, first):
        correlate(
            0, first, (vh[:, 256:512], vl[:, 256:512]), (vh[:, 0:256], vl[:, 0:256]), NT
        )

    def load_rows(ref):
        for a, b, p in combos:
            top = (a * 2 + b) * 128
            high, low = split(ref[pl.ds(sub(a, b, p), 128, stride=8), :])
            wh[top:top + 128, p * 128:p * 128 + 128] = high
            wl[top:top + 128, p * 128:p * 128 + 128] = low

    def grad_rows(layer, first):
        correlate(layer, first, (wh[256:512], wl[256:512]), (wh[0:256], wl[0:256]), TN)

    f1_bits = f1.reshape(K, 2, 32, 2, 8, 128)
    xb_bits = xb.reshape(2, 32, 2, 8, 128)
    group = lax.broadcasted_iota(jnp.int32, (256, 128), 1) // 32

    def middle(k, first):
        parts = [f1_bits[k, i // 2, :, i % 2].reshape(256, 128) for i in range(4)]
        for j in range(4):
            turned = [
                parts[i] if i == j else pltpu.roll(parts[i], ((i - j) % 4) * 32, 1)
                for i in range(4)
            ]
            low_half = jnp.where(group == 0, turned[0], turned[1])
            high_half = jnp.where(group == 2, turned[2], turned[3])
            value = jnp.where(group < 2, low_half, high_half)
            xb_bits[j // 2, :, j % 2] = value.reshape(32, 8, 128)
        load_rows(xb)
        value = dot3(mats[1], wh[...], wl[...], NT)
        for a, b, p in combos:
            left = (a * 2 + b) * 128
            zb[pl.ds(sub(a, b, p), 128, stride=8), :] = (
                value[p * 128:p * 128 + 128, left:left + 128]
            )
        grad_rows(1, first)
        load_rows(zb)
        both = lax.dot_general(wh[...], mats[2], NT, preferred_element_type=F32)
        rest = lax.dot_general(wl[...], mats[2, 0:256], NT, preferred_element_type=F32)
        value = both[:, 0:256] + (both[:, 256:512] + rest)
        for a, b, p in combos:
            top = (a * 2 + b) * 128
            s2[k, pl.ds(sub(a, b, p), 128, stride=8), :] = (
                value[top:top + 128, p * 128:p * 128 + 128]
            )

    def finish(k):
        for a, b, p in combos:
            outs[a][pl.ds(k * 4 + b * 2 + p, 128, stride=16), :] = (
                f2[k, pl.ds(sub(a, b, p), 128, stride=8), :].T
            )

    def tiles(ref):
        return ref.reshape(K, 4, PLANE, 8, 128)

    def plane_start(st, src, dst, k, where=bulk):
        src_t, dst_t = tiles(src), tiles(dst)
        for offset in where:
            q = peer(*offset)
            remote(
                src_t.at[k, :, q], dst_t.at[k, :, m],
                st_send.at[st, k], st_recv.at[st, k], y * PLANE + q,
            ).start()
        if where[-1] == (0, 0, 1):
            own = pltpu.make_async_copy(src_t.at[k, :, m], dst_t.at[k, :, m], own_sem.at[st, k])
            own.start()

    def plane_wait(st, src, dst, k, arrived=True):
        whole = remote(
            src.at[k, pl.ds(0, 992)], dst.at[k, pl.ds(0, 992)],
            st_send.at[st, k], st_recv.at[st, k], partner,
        )
        if not arrived:
            whole.wait_send()
            return
        whole.wait_recv()
        src_t, dst_t = tiles(src), tiles(dst)
        pltpu.make_async_copy(src_t.at[k, :, m], dst_t.at[k, :, m], own_sem.at[st, k]).wait()

    def y_start(st, src, dst, k):
        src_t, dst_t = tiles(src), tiles(dst)
        for step in (2, 1, 3):
            to = lax.rem(y + step, 4)
            remote(
                src_t.at[k, to], dst_t.at[k, y],
                st_send.at[st, k], st_recv.at[st, k], to * PLANE + m,
            ).start()
        pltpu.make_async_copy(src_t.at[k, y], dst_t.at[k, y], own_sem.at[st, k]).start()

    def y_wait(st, src, dst, k, arrived=True):
        whole = remote(
            src.at[k, pl.ds(0, 768)], dst.at[k, pl.ds(0, 768)],
            st_send.at[st, k], st_recv.at[st, k], partner,
        )
        if not arrived:
            whole.wait_send()
            return
        whole.wait_recv()
        src_t, dst_t = tiles(src), tiles(dst)
        pltpu.make_async_copy(src_t.at[k, y], dst_t.at[k, y], own_sem.at[st, k]).wait()

    buffers = ((s1, r1), (r1, f1), (s2, r2), (r2, f2))
    y_stage = [[k % 2 == (0 if st in (0, 3) else 1) for k in range(K)] for st in range(4)]

    def go(st, k):
        (y_start if y_stage[st][k] else plane_start)(st, *buffers[st], k)

    def got(st, k, arrived=True):
        (y_wait if y_stage[st][k] else plane_wait)(st, *buffers[st], k, arrived)

    def red(step, layer, src, dst, device):
        return remote(
            src, dst, red_send.at[step, layer], red_recv.at[step, layer], device
        )

    mine = pl.ds((core * 16 + chip) * 8, 8)
    slot = pl.ds(chip * 8, 8)
    y_slot = pl.ds(y * 8, 8)
    own_half = pl.ds(core * 128, 128)
    other_half = pl.ds((1 - core) * 128, 128)

    def pair_copy(layer):
        return red(0, layer, terms.at[layer, other_half], cb.at[layer], partner)

    def back_copy(layer):
        return red(4, layer, gout.at[layer, own_half], gout.at[layer, own_half], partner)

    def all_of(step, layer):
        if step == 0:
            return pair_copy(layer)
        if step == 1:
            part = pl.ds(0, 120)
            return red(1, layer, hb.at[layer, part], mr.at[layer, part], partner)
        if step == 2:
            part = pl.ds(0, 24)
            return red(2, layer, yb.at[layer, part], yb.at[layer, part], partner)
        if step == 3:
            part = pl.ds(0, 120)
            return red(3, layer, gout.at[layer, part], gout.at[layer, part], partner)
        return back_copy(layer)

    def reduce0(layer):
        real = acc[layer, 0:128, 0:128] + acc[layer, 128:256, 128:256]
        imag = acc[layer, 128:256, 0:128] - acc[layer, 0:128, 128:256]
        high, low = split(jnp.concatenate([real, -imag], axis=1))
        left = lax.dot_general(high, mats[layer], NT, preferred_element_type=F32)
        rest = lax.dot_general(low, mats[layer, 0:256], NT, preferred_element_type=F32)
        value = left[:, 0:256] + (left[:, 256:512] + rest)
        terms[layer, 0:128, :] = value[:, 0:128]
        terms[layer, 128:256, :] = -value[:, 128:256]
        pair_copy(layer).start()

    def reduce1(layer):
        all_of(0, layer).wait_recv()
        hb[layer] = terms[layer, own_half, :] + cb[layer]
        mr[layer, slot, :] = hb[layer, slot, :]
        for offset in same_core:
            q = peer(*offset)
            red(
                1, layer, hb.at[layer, pl.ds((q // 2) * 8, 8)], mr.at[layer, slot],
                y * PLANE + q,
            ).start()

    def reduce2(layer):
        all_of(1, layer).wait_recv()
        parts = [mr[layer, i * 8:i * 8 + 8, :] for i in range(16)]
        while len(parts) > 1:
            parts = [parts[i] + parts[i + 1] for i in range(0, len(parts), 2)]
        yb[layer, y_slot, :] = parts[0]
        for step in (2, 1, 3):
            red(
                2, layer, yb.at[layer, y_slot], yb.at[layer, y_slot],
                lax.rem(y + step, 4) * PLANE + m,
            ).start()

    def reduce3(layer):
        all_of(2, layer).wait_recv()
        total = (yb[layer, 0:8, :] + yb[layer, 8:16, :]) + (
            yb[layer, 16:24, :] + yb[layer, 24:32, :]
        )
        gout[layer, mine, :] = total * scale
        for offset in same_core:
            red(
                3, layer, gout.at[layer, mine], gout.at[layer, mine],
                y * PLANE + peer(*offset),
            ).start()

    def reduce4(layer):
        all_of(3, layer).wait_recv()
        back_copy(layer).start()

    def reduce5(layer):
        all_of(4, layer).wait_recv()

    loads[0].wait()
    build(0)
    loads[1].wait()
    loads[2].wait()
    gate0(1, True)
    pl.semaphore_wait(barrier, len(near))
    tell(entry_sem.at[0], rounds[0])
    plane_start(0, s1, r1, 1, known[0])
    grad0(1, True)
    gate0(0, False)
    go(0, 0)
    hear(0)
    tell(entry_sem.at[1], rounds[1])
    plane_start(0, s1, r1, 1, known[1])
    grad0(0, False)
    gate0(2, False)
    go(0, 2)
    hear(1)
    plane_start(0, s1, r1, 1, known[2])
    grad0(2, False)
    gate0(3, False)
    go(0, 3)
    grad0(3, False)
    loads[3].wait()
    build(1)
    build(2)
    reduce0(0)
    got(0, 0)
    go(1, 0)
    reduce1(0)
    got(0, 1)
    go(1, 1)
    got(0, 2)
    go(1, 2)
    got(0, 3)
    go(1, 3)
    got(1, 1)
    middle(1, True)
    go(2, 1)
    grad_rows(2, True)
    got(1, 0)
    middle(0, False)
    go(2, 0)
    grad_rows(2, False)
    reduce2(0)
    got(1, 3)
    middle(3, False)
    go(2, 3)
    grad_rows(2, False)
    got(1, 2)
    middle(2, False)
    go(2, 2)
    grad_rows(2, False)
    reduce0(2)
    reduce0(1)
    reduce1(2)
    reduce1(1)
    got(2, 1)
    go(3, 1)
    reduce3(0)
    got(2, 0)
    go(3, 0)
    reduce2(2)
    reduce2(1)
    got(2, 3)
    go(3, 3)
    got(2, 2)
    go(3, 2)
    reduce3(2)
    reduce3(1)
    reduce4(0)
    got(3, 1)
    finish(1)
    got(3, 0)
    finish(0)
    reduce4(2)
    reduce4(1)
    got(3, 2)
    finish(2)
    got(3, 3)
    finish(3)
    for layer in range(3):
        reduce5(layer)

    for st in range(4):
        for k in range(K):
            got(st, k, False)
    for step in range(5):
        for layer in range(3):
            all_of(step, layer).wait_send()


def store_kernel(psi_res, lam_res, gout, psi_out, lam_out, grad_out, sem):
    copies = [
        pltpu.make_async_copy(src, dst, sem.at[i])
        for i, (src, dst) in enumerate(((psi_res, psi_out), (lam_res, lam_out), (gout, grad_out)))
    ]
    for copy in copies:
        copy.start()
    for copy in copies:
        copy.wait()


def rows_of(field):
    return field.reshape(2, 1024, 128).transpose(1, 0, 2).reshape(2048, 128)


def field_of(rows):
    return rows.reshape(1024, 2, 128).transpose(1, 0, 2).reshape(2, 131072)


def on_device(state, costate, gates):
    scale = 1.0 / math.sqrt(128 * 1024)
    dma = pltpu.SemaphoreType.DMA
    shapes = ((2048, 128), (2048, 128), (3, 256, 128))
    results = pl.pallas_call(
        functools.partial(kernel, scale),
        out_shape=tuple(pltpu.VMEM(shape, F32) for shape in shapes),
        in_specs=[pl.BlockSpec(memory_space=pl.ANY)] * 3,
        out_specs=[pl.BlockSpec(memory_space=pltpu.VMEM)] * 3,
        scratch_shapes=[
            pltpu.VMEM((2048, 128), F32),
            pltpu.VMEM((2048, 128), F32),
            pltpu.VMEM((768, 128), F32),
            pltpu.VMEM((3, 512, 256), BF16),
        ]
        + [pltpu.VMEM((K, 1024, 128), F32)] * 6
        + [
            pltpu.VMEM((1024, 128), F32),
            pltpu.VMEM((1024, 128), F32),
            pltpu.VMEM((256, 512), BF16),
            pltpu.VMEM((256, 512), BF16),
            pltpu.VMEM((512, 256), BF16),
            pltpu.VMEM((512, 256), BF16),
            pltpu.VMEM((3, 256, 256), F32),
            pltpu.VMEM((3, 256, 128), F32),
            pltpu.VMEM((3, 128, 128), F32),
            pltpu.VMEM((3, 128, 128), F32),
            pltpu.VMEM((3, 128, 128), F32),
            pltpu.VMEM((3, 32, 128), F32),
            dma((4,)), pltpu.SemaphoreType.REGULAR((2,)),
            dma((4, K)), dma((4, K)), dma((4, K)), dma((5, 3)), dma((5, 3)),
        ],
        compiler_params=pltpu.CompilerParams(collective_id=0, has_side_effects=True),
        name="window",
    )(rows_of(state), rows_of(costate), gates.reshape(768, 128))
    psi, lam, grads = pl.pallas_call(
        store_kernel,
        out_shape=tuple(jax.ShapeDtypeStruct(shape, F32) for shape in shapes),
        in_specs=[pl.BlockSpec(memory_space=pltpu.VMEM)] * 3,
        out_specs=[pl.BlockSpec(memory_space=pl.ANY)] * 3,
        scratch_shapes=[dma((3,))],
        name="store",
    )(*(pltpu.with_memory_space_constraint(r, pltpu.VMEM) for r in results))
    return field_of(psi), field_of(lam), grads.reshape(3, 2, 128, 128)


def solution(mesh):
    return jax.shard_map(
        on_device,
        mesh=mesh,
        in_specs=(P(None, "amp"), P(None, "amp"), P()),
        out_specs=(P(None, "amp"), P(None, "amp"), P()),
        check_vma=False,
    )
```
